256 devices in a mesh: tm: 16 (over z, core), space: 16 (over x, y).
Axes of the slice: x: 4, y: 4, z: 8, core: 2. Of those that a mesh axis runs over, the one named last changes fastest.
Arguments:
- features: bfloat16 [64, 256, 128, 128], P('tm', 'space'), may hold values from -6 to 6
- kernel_first: bfloat16 [3, 3, 3, 128, 128], replicated, may hold values from -0.109375 to 0.109375
- bias_first: float32 [128], replicated, may hold values from -3 to 3
- kernel_down: bfloat16 [3, 3, 128, 256], replicated, may hold values from -0.1875 to 0.1875
- bias_down: float32 [256], replicated, may hold values from -3 to 3
- kernel_second: bfloat16 [3, 3, 3, 256, 256], replicated, may hold values from -0.078125 to 0.078125
- bias_second: float32 [256], replicated, may hold values from -3 to 3
Outputs:
- latent: bfloat16 [64, 128, 64, 256], P('tm', 'space')
The draws below stay inside these ranges and needn't reach their ends.
All inputs are finite; a program needn't handle non-finite values.
Results may differ from the reference program's by a relative error of at most 0.0095.
Values may be sent and summed in bfloat16 or wider, within the bound.
No kernel may reach another device: no remote copies, remote signals or barrier semaphores. Data moves between devices by JAX's collectives and lax.ppermute only.
A program may use at most 64 MiB of HBM per device.

```python
import jax
import jax.numpy as jnp
from jax import lax

C0 = 128
C1 = 256
COLS = 128
FRAMES = 64
ROWS = 256


def block_levels(stream_key, shape, shards, low, largest):
    def one(dim, shards_of):
        draws = jax.random.uniform(jax.random.fold_in(jax.random.fold_in(stream_key, 6), dim), (shards_of,), jnp.float32, low / len(shards), largest / len(shards))
        return jnp.repeat(jnp.exp(draws), shape[dim] // shards_of).reshape((-1,) + (1,) * (len(shape) - dim - 1))

    loudness = one(*shards[0])
    for cut in shards[1:]:
        loudness = loudness * one(*cut)
    return loudness


def scatter_about(own_key, shape, spread, most, split=(), held_as=jnp.bfloat16):
    drawn = spread * jax.random.normal(own_key, shape, jnp.float32)
    if split:
        drawn = drawn * block_levels(own_key, shape, split, -0.22, 0.18)
    return jnp.clip(drawn, -most, most).astype(held_as)


def setup_inputs(seed: int = 0) -> dict:
    arg_keys = jax.random.split(jax.random.key(seed), 8)
    features = scatter_about(arg_keys[0], (FRAMES, ROWS, COLS, C0), 1.0, 6.0, ((0, 16), (1, 16)))
    kernel_first = scatter_about(arg_keys[1], (3, 3, 3, C0, C0), (27 * C0) ** -0.5, 0.109375)
    bias_first = scatter_about(arg_keys[2], (C0,), 0.5, 3.0, (), jnp.float32)
    kernel_down = scatter_about(arg_keys[3], (3, 3, C0, C1), (9 * C0) ** -0.5, 0.1875)
    bias_down = scatter_about(arg_keys[4], (C1,), 0.5, 3.0, (), jnp.float32)
    kernel_second = scatter_about(arg_keys[5], (3, 3, 3, C1, C1), (27 * C1) ** -0.5, 0.078125)
    bias_second = scatter_about(arg_keys[6], (C1,), 0.5, 3.0, (), jnp.float32)
    return {"features": features, "kernel_first": kernel_first, "bias_first": bias_first, "kernel_down": kernel_down, "bias_down": bias_down, "kernel_second": kernel_second, "bias_second": bias_second}


def conv_causal(activated, weight):
    activated = lax.optimization_barrier(activated)
    inputs = activated.astype(jnp.float32)[None]
    result = lax.conv_general_dilated(inputs, weight.astype(jnp.float32), (1, 1, 1), ((2, 0), (1, 1), (1, 1)), dimension_numbers=("NDHWC", "DHWIO", "NDHWC"), precision=lax.Precision.HIGHEST)
    return result[0]


def reference(features, kernel_first, bias_first, kernel_down, bias_down, kernel_second, bias_second):
    act_in = jax.nn.silu(features.astype(jnp.float32)).astype(jnp.bfloat16)
    first_out = (features.astype(jnp.float32) + bias_first + conv_causal(act_in, kernel_first)).astype(jnp.bfloat16)
    first_out = lax.optimization_barrier(first_out)
    reduced = lax.conv_general_dilated(first_out.astype(jnp.float32), kernel_down.astype(jnp.float32), (2, 2), ((1, 1), (1, 1)), dimension_numbers=("NHWC", "HWIO", "NHWC"), precision=lax.Precision.HIGHEST)
    reduced = (reduced + bias_down).astype(jnp.bfloat16)
    reduced = lax.optimization_barrier(reduced)
    act_mid = jax.nn.silu(reduced.astype(jnp.float32)).astype(jnp.bfloat16)
    latent = (reduced.astype(jnp.float32) + bias_second + conv_causal(act_mid, kernel_second)).astype(jnp.bfloat16)
    return latent
```

```python
import functools

import jax
import jax.numpy as jnp
from jax import lax
from jax.experimental import pallas as pl
from jax.experimental.pallas import tpu as pltpu
from jax.sharding import PartitionSpec as P

BF = jnp.bfloat16
F32 = jnp.float32
VMEM = pltpu.VMEM
LIMIT = 24 * 2**20


def silu(v):
    h = 0.5 * v
    return h + h * jnp.tanh(h)


def prep_row(x, s_ref, q_ref):
    q_ref[...] = x
    even = q_ref[pl.ds(0, 64, stride=2), :]
    odd = q_ref[pl.ds(1, 64, stride=2), :]
    d1 = silu(even)
    d2 = silu(odd)
    s_ref[0, 8:72] = d1
    s_ref[1, 8:72] = d2
    d3 = s_ref[0, 9:73]
    d0 = s_ref[1, 7:71]
    return even, odd, (d0 - d2, d1 + d2, d2 - d1, d1 - d3)


def clear_edges(s_ref):
    for f in range(s_ref.shape[0]):
        for e in range(2):
            s_ref[f, e, 0:8] = jnp.zeros((8, s_ref.shape[-1]), F32)
            s_ref[f, e, s_ref.shape[2] - 8 :] = jnp.zeros((8, s_ref.shape[-1]), F32)


def transformed(g0, g1, g2):
    half = 0.5 * (g0 + g2)
    return half + 0.5 * g1, half - 0.5 * g1


def kernel_p(x_ref, kf_ref, ks_ref, u_ref, x2_ref, w_ref, g_ref, s_ref, q_ref):
    clear_edges(s_ref)

    def row(r, carry):
        for f in range(4):
            x = x_ref[f, r].astype(F32)
            even, odd, us = prep_row(x, s_ref.at[f], q_ref.at[f])
            lanes = slice((f % 2) * 128, (f % 2) * 128 + 128)
            for k in range(4):
                u_ref[k, f // 2, r + 2, :, lanes] = us[k].astype(BF)
            x2_ref[f, r + 1, :, 0:128] = even.astype(BF)
            x2_ref[f, r + 1, :, 128:256] = odd.astype(BF)
        return carry

    lax.fori_loop(0, 16, row, 0)

    def wrow(j, carry):
        zero = jnp.zeros((128, 128), BF)
        for i in range(3):
            g0, g1, g2 = (kf_ref[i, j, c] for c in range(3))
            a, b = transformed(g0.astype(F32), g1.astype(F32), g2.astype(F32))
            for k, g in enumerate((g0, a.astype(BF), b.astype(BF), g2)):
                if i == 0:
                    w_ref[k, j, 0, 0:128, 0:128] = g
                    w_ref[k, j, 0, 128:256, 128:256] = g
                    w_ref[k, j, 0, 0:128, 128:256] = zero
                    w_ref[k, j, 1, 128:256, 0:128] = zero
                elif i == 1:
                    w_ref[k, j, 0, 128:256, 0:128] = g
                    w_ref[k, j, 1, 0:128, 128:256] = g
                else:
                    w_ref[k, j, 1, 0:128, 0:128] = g
                    w_ref[k, j, 1, 128:256, 128:256] = g
        return carry

    lax.fori_loop(0, 3, wrow, 0)

    def grow(n, carry):
        i, j = n // 3, n % 3
        a, b = transformed(*(ks_ref[i, j, c].astype(F32) for c in range(3)))
        g_ref[0, n] = a.astype(BF)
        g_ref[1, n] = b.astype(BF)
        return carry

    lax.fori_loop(0, 9, grow, 0)


def conv_down(u_ref, w_ref, kd_ref, f_ref, o_ref, pairs, above, residual, bias):
    for q in range(2):
        for g in range(17):
            o_ref[q, g, 0:8] = jnp.zeros((8, 128), F32)
    for g0, rows in ((0, 8), (8, 9)):
        ms = []
        for k in range(4):
            lhs = jnp.concatenate(
                [u_ref[k, p, g0 + j : g0 + j + rows].reshape(rows * 64, 256) for j in range(3) for p, _ in pairs],
                axis=1,
            )
            rhs = jnp.concatenate([w_ref[k, j, which] for j in range(3) for _, which in pairs], axis=0)
            ms.append(jnp.dot(lhs, rhs, preferred_element_type=F32))
        both = (ms[1] + ms[2] + ms[0], ms[1] - ms[2] - ms[3])
        for q in range(2):
            for e in range(2):
                y = both[e][:, q * 128 : q * 128 + 128].reshape(rows, 64, 128)
                if residual is not None:
                    y = y + residual[q, g0 : g0 + rows, :, e * 128 : e * 128 + 128].astype(F32) + bias
                for n in range(rows):
                    g = g0 + n
                    row = y[n] * above if g == 0 else y[n]
                    f_ref[q, g % 2, g // 2, :, e * 128 : e * 128 + 128] = row.astype(BF)
                    if e == 1:
                        o_ref[q, g, 8:72] = row
                        f_ref[q, g % 2, g // 2, :, 256:384] = o_ref[q, g, 7:71].astype(BF)
    rhs = jnp.concatenate([kd_ref[j, c] for j in range(3) for c in (1, 2, 0)], axis=0)
    out = []
    for q in range(2):
        lhs = jnp.concatenate(
            [
                f_ref[q, 0, 0:8].reshape(512, 384),
                f_ref[q, 1, 0:8].reshape(512, 384),
                f_ref[q, 0, 1:9].reshape(512, 384),
            ],
            axis=1,
        )
        out.append(jnp.dot(lhs, rhs, preferred_element_type=F32))
    return out


def kernel_a(ok_ref, u_in, x2_in, top_ref, bot_ref, w_ref, kd_ref, u_ref, x2_ref, part_ref, s_ref, q_ref, f_ref, o_ref):
    clear_edges(s_ref)
    for n in range(3):
        for f in range(4):
            x = (top_ref[f, n] if n < 2 else bot_ref[f, 0]).astype(F32)
            even, odd, us = prep_row(x, s_ref.at[f], q_ref.at[f])
            lanes = slice((f % 2) * 128, (f % 2) * 128 + 128)
            for k in range(4):
                u_ref[k, f // 2, (0, 1, 18)[n], :, lanes] = us[k].astype(BF)
            if n == 1:
                x2_ref[f, 0, :, 0:128] = even.astype(BF)
                x2_ref[f, 0, :, 128:256] = odd.astype(BF)
    above = ok_ref[0].astype(F32)
    out = conv_down(u_ref, w_ref, kd_ref, f_ref, o_ref, ((1, 0),), above, None, None)
    for q in range(2):
        part_ref[q] = out[q].reshape(8, 64, 256).astype(BF)


def finish(q, red, red_ref, act_ref):
    r16 = red.astype(BF)
    red_ref[q] = r16.reshape(8, 64, 256)
    act_ref[q] = silu(r16.astype(F32)).astype(BF).reshape(8, 64, 256)


def kernel_b(ok_ref, u_ref, x2_ref, w_ref, kd_ref, bf_ref, bd_ref, red_ref, act_ref, dn_ref, up_ref, f_ref, o_ref):
    above = ok_ref[0].astype(F32)
    out = conv_down(u_ref, w_ref, kd_ref, f_ref, o_ref, ((0, 0), (1, 1)), above, x2_ref.at[2:4], bf_ref[...])
    for q in range(2):
        finish(q, out[q] + bd_ref[...], red_ref, act_ref)
        dn_ref[q] = act_ref[q, 7]
        up_ref[q] = act_ref[q, 0]


def kernel_c(
    ok_ref, u_ref, x2_ref, w_ref, kd_ref, bf_ref, bd_ref, z_ref, dn_in, up_in, red_ref, act_ref, dn_ref, up_ref, f_ref, o_ref
):
    above = ok_ref[0].astype(F32)
    out = conv_down(u_ref, w_ref, kd_ref, f_ref, o_ref, ((0, 1),), above, x2_ref.at[0:2], bf_ref[...])
    for q in range(2):
        finish(q, out[q] + bd_ref[...] + z_ref[q].reshape(512, 256).astype(F32), red_ref, act_ref)
        dn_ref[q] = act_ref[q, 7]
        up_ref[q] = act_ref[q, 0]
        dn_ref[2 + q] = dn_in[q]
        up_ref[2 + q] = up_in[q]


def prep_mid(row, s_ref, q_ref):
    x = row.astype(F32)
    q_ref[0] = x[:, 0:128]
    q_ref[1] = x[:, 128:256]
    d1 = jnp.concatenate([q_ref[h, pl.ds(0, 32, stride=2), :] for h in range(2)], axis=1)
    d2 = jnp.concatenate([q_ref[h, pl.ds(1, 32, stride=2), :] for h in range(2)], axis=1)
    s_ref[0, 8:40] = d1
    s_ref[1, 8:40] = d2
    d3 = s_ref[0, 9:41]
    d0 = s_ref[1, 7:39]
    return (d0 - d2, d1 + d2, d2 - d1, d1 - d3)


def conv_mid(slab, ks_ref, g_ref, red_ref, bias, t_ref, out_ref):
    ms = []
    for k in range(4):
        lhs = jnp.concatenate([slab(k, i, j) for i in range(3) for j in range(3)], axis=1)
        if k == 0 or k == 3:
            rhs = jnp.concatenate([ks_ref[i, j, 2 * (k // 3)] for i in range(3) for j in range(3)], axis=0)
        else:
            rhs = g_ref[k - 1].reshape(2304, 256)
        ms.append(jnp.dot(lhs, rhs, preferred_element_type=F32))
    y0 = (ms[1] + ms[2] + ms[0]).reshape(16, 32, 256)
    y1 = (ms[1] - ms[2] - ms[3]).reshape(16, 32, 256)
    for n in range(16):
        for h in range(2):
            lanes = slice(h * 128, h * 128 + 128)
            t_ref[n, h, pl.ds(0, 32, stride=2), :] = y0[n, :, lanes]
            t_ref[n, h, pl.ds(1, 32, stride=2), :] = y1[n, :, lanes]
            v = t_ref[n, h] + red_ref[n // 8, n % 8, :, lanes].astype(F32) + bias[:, lanes]
            out_ref[n // 8, n % 8, :, lanes] = v.astype(BF)


def kernel_ma(
    act01_ref, act23_ref, top_ref, bot_ref, ks_ref, g_ref, red_ref, bs_ref, lat_ref, u2_ref, v2_ref, s_ref, q_ref, t_ref, out_ref, sem
):
    clear_edges(s_ref)

    def row(r, carry):
        for f in range(4):
            src = (act01_ref, act23_ref)[f // 2]
            us = prep_mid(src[f % 2, r], s_ref.at[f], q_ref.at[f])
            dst = (u2_ref, v2_ref)[f // 2]
            for k in range(4):
                dst[k, f % 2, r + 1] = us[k].astype(BF)
        return carry

    lax.fori_loop(0, 8, row, 0)
    for f in range(4):
        dst = (u2_ref, v2_ref)[f // 2]
        for ref, at in ((top_ref, 0), (bot_ref, 9)):
            us = prep_mid(ref[f], s_ref.at[f], q_ref.at[f])
            for k in range(4):
                dst[k, f % 2, at] = us[k].astype(BF)

    def slab(k, i, j):
        if i == 0:
            return u2_ref[k, :, j : j + 8].reshape(512, 256)
        if i == 2:
            return v2_ref[k, :, j : j + 8].reshape(512, 256)
        return jnp.concatenate(
            [u2_ref[k, 1, j : j + 8].reshape(256, 256), v2_ref[k, 0, j : j + 8].reshape(256, 256)], axis=0
        )

    conv_mid(slab, ks_ref, g_ref, red_ref, bs_ref[...], t_ref, out_ref)
    copy = pltpu.make_async_copy(out_ref, lat_ref.at[2:4], sem)
    copy.start()
    copy.wait()


def kernel_mb(
    lat_in, zact_ref, ztop_ref, zbot_ref, u2_ref, ks_ref, g_ref, red_ref, bs_ref, lat_ref, v2_ref, s_ref, q_ref, t_ref, out_ref, sem
):
    clear_edges(s_ref)

    def row(r, carry):
        for f in range(2):
            us = prep_mid(zact_ref[f, r], s_ref.at[f], q_ref.at[f])
            for k in range(4):
                v2_ref[k, f, r + 1] = us[k].astype(BF)
        return carry

    lax.fori_loop(0, 8, row, 0)
    for f in range(2):
        for ref, at in ((ztop_ref, 0), (zbot_ref, 9)):
            us = prep_mid(ref[f], s_ref.at[f], q_ref.at[f])
            for k in range(4):
                v2_ref[k, f, at] = us[k].astype(BF)

    def slab(k, i, j):
        if i == 0:
            return v2_ref[k, :, j : j + 8].reshape(512, 256)
        if i == 2:
            return u2_ref[k, :, j : j + 8].reshape(512, 256)
        return jnp.concatenate(
            [v2_ref[k, 1, j : j + 8].reshape(256, 256), u2_ref[k, 0, j : j + 8].reshape(256, 256)], axis=0
        )

    conv_mid(slab, ks_ref, g_ref, red_ref, bs_ref[...], t_ref, out_ref)
    copy = pltpu.make_async_copy(out_ref, lat_ref.at[0:2], sem)
    copy.start()
    copy.wait()


V = pl.BlockSpec(memory_space=pltpu.VMEM)
ANY = pl.BlockSpec(memory_space=pl.ANY)
SM = pl.BlockSpec(memory_space=pltpu.SMEM)


def sds(*shape):
    return jax.ShapeDtypeStruct(shape, BF)


def res(*shape):
    return VMEM(shape, BF)


def keep(*xs):
    return [pltpu.with_memory_space_constraint(x, pltpu.VMEM) for x in xs]


def call(body, name, ins, outs, scratch, flops, in_specs=None, out_specs=None, aliases=None):
    return pl.pallas_call(
        body,
        out_shape=outs,
        in_specs=in_specs or [V] * len(ins),
        out_specs=out_specs or [V] * len(outs),
        scratch_shapes=scratch,
        input_output_aliases=aliases or {},
        compiler_params=pltpu.CompilerParams(vmem_limit_bytes=LIMIT),
        cost_estimate=pl.CostEstimate(flops=flops, bytes_accessed=4 << 20, transcendentals=0),
        name=name,
    )(*ins)


def on_device(features, kf, bf, kd, bd, ks, bs):
    tm, sp = lax.axis_size("tm"), lax.axis_size("space")
    down = [(i, i + 1) for i in range(sp - 1)]
    up = [(i + 1, i) for i in range(sp - 1)]
    later = [(i, i + 1) for i in range(tm - 1)]
    cross = lambda step: [
        (t * sp + s, (t + 1) * sp + s + step) for t in range(tm - 1) for s in range(sp) if 0 <= s + step < sp
    ]
    top = lax.ppermute(features[:, 14:16], "space", down)
    bot = lax.ppermute(features[:, 0:1], "space", up)
    ok = (lax.axis_index("space") > 0).astype(jnp.int32).reshape(1)
    bf2, bd2, bs2 = bf.reshape(1, 128), bd.reshape(1, 256), bs.reshape(1, 256)

    prep = [VMEM((4, 2, 80, 128), F32), VMEM((4, 128, 128), F32)]
    mid = [VMEM((2, 2, 9, 64, 384), BF), VMEM((2, 17, 72, 128), F32)]
    u, x2, w, g = call(
        kernel_p, "prep", (features, kf, ks),
        [res(4, 2, 19, 64, 256), res(4, 17, 64, 256), res(4, 3, 2, 256, 256), res(2, 9, 256, 256)],
        prep, 2_000_000_000,
    )
    u, x2, part = call(
        kernel_a, "ahead", (ok, *keep(u, x2), top, bot, *keep(w), kd),
        [res(4, 2, 19, 64, 256), res(4, 17, 64, 256), sds(2, 8, 64, 256)],
        prep + mid, 2_500_000_000, in_specs=[SM] + [V] * 6, aliases={1: 0, 2: 1},
    )
    zpart = lax.ppermute(part, "tm", later)
    red23, act23, dn23, up23 = call(
        kernel_b, "late", (ok, *keep(u, x2, w), kd, bf2, bd2),
        [res(2, 8, 64, 256), sds(2, 8, 64, 256), sds(2, 64, 256), sds(2, 64, 256)],
        mid, 4_000_000_000, in_specs=[SM] + [V] * 6,
    )
    zact = lax.ppermute(act23, "tm", later)
    ztop = lax.ppermute(dn23, ("tm", "space"), cross(1))
    zbot = lax.ppermute(up23, ("tm", "space"), cross(-1))
    red01, act01, dn, ups = call(
        kernel_c, "early", (ok, *keep(u, x2, w), kd, bf2, bd2, zpart, dn23, up23),
        [res(2, 8, 64, 256), res(2, 8, 64, 256), sds(4, 64, 256), sds(4, 64, 256)],
        mid, 2_500_000_000, in_specs=[SM] + [V] * 9,
    )
    atop = lax.ppermute(dn, "space", down)
    abot = lax.ppermute(ups, "space", up)

    tail = [VMEM((16, 2, 64, 128), F32), VMEM((2, 8, 64, 256), BF), pltpu.SemaphoreType.DMA]
    lat, u2 = call(
        kernel_ma, "mid_late", (*keep(act01), act23, atop, abot, ks, *keep(g, red23), bs2),
        [sds(4, 8, 64, 256), res(4, 2, 10, 32, 256)],
        [VMEM((4, 2, 10, 32, 256), BF), VMEM((4, 2, 48, 256), F32), VMEM((4, 2, 64, 128), F32)] + tail,
        3_000_000_000, out_specs=[ANY, V],
    )
    (lat,) = call(
        kernel_mb, "mid_early", (lat, zact, ztop, zbot, *keep(u2), ks, *keep(g, red01), bs2),
        [sds(4, 8, 64, 256)],
        [VMEM((4, 2, 10, 32, 256), BF), VMEM((2, 2, 48, 256), F32), VMEM((2, 2, 64, 128), F32)] + tail,
        3_000_000_000, in_specs=[ANY] + [V] * 8, out_specs=[ANY], aliases={0: 0},
    )
    return lat


def solution(mesh):
    in_specs = (P("tm", "space", None, None), P(), P(), P(), P(), P(), P())
    out_specs = P("tm", "space", None, None)
    return jax.shard_map(on_device, mesh=mesh, in_specs=in_specs, out_specs=out_specs, check_vma=False)
```

```python
import jax
import jax.numpy as jnp
from jax import lax
from jax.experimental import pallas as pl
from jax.experimental.pallas import tpu as pltpu
from jax.sharding import PartitionSpec as P

BF = jnp.bfloat16
F32 = jnp.float32
VMEM = pltpu.VMEM
LIMIT = 24 * 2**20


def silu(v):
    h = 0.5 * v
    return h + h * jnp.tanh(h)


def clear_edges(s_ref):
    for f in range(s_ref.shape[0]):
        for e in range(2):
            s_ref[f, e, 0:8] = jnp.zeros((8, s_ref.shape[-1]), F32)
            s_ref[f, e, s_ref.shape[2] - 8 :] = jnp.zeros((8, s_ref.shape[-1]), F32)


def prep_first(x, f, r, u_ref, x2_ref, s_ref, q_ref, residual=True):
    q_ref[f] = x.astype(F32)
    even = q_ref[f, pl.ds(0, 64, stride=2), :]
    odd = q_ref[f, pl.ds(1, 64, stride=2), :]
    d1 = silu(even)
    d2 = silu(odd)
    s_ref[f, 0, 8:72] = d1
    s_ref[f, 1, 8:72] = d2
    d3 = s_ref[f, 0, 9:73]
    d0 = s_ref[f, 1, 7:71]
    lanes = slice((f % 2) * 128, (f % 2) * 128 + 128)
    for k, v in enumerate((d0 - d2, d1 + d2, d2 - d1, d1 - d3)):
        u_ref[k, f // 2, r + 1, :, lanes] = v.astype(BF)
    if residual:
        x2_ref[f, r, :, 0:128] = even.astype(BF)
        x2_ref[f, r, :, 128:256] = odd.astype(BF)


def transformed(g0, g1, g2):
    half = 0.5 * (g0 + g2)
    return half + 0.5 * g1, half - 0.5 * g1


def first_rows(u_ref, w_ref, f_ref, o_ref, pairs, g0, rows, below, residual, bias):
    ms = []
    for k in range(4):
        lhs = jnp.concatenate(
            [u_ref[k, p, g0 + j : g0 + j + rows].reshape(rows * 64, 256) for j in range(3) for p, _ in pairs], axis=1
        )
        rhs = jnp.concatenate([w_ref[k, j, which] for j in range(3) for _, which in pairs], axis=0)
        ms.append(jnp.dot(lhs, rhs, preferred_element_type=F32))
    both = (ms[1] + ms[2] + ms[0], ms[1] - ms[2] - ms[3])
    for q in range(2):
        for e in range(2):
            lanes = slice(e * 128, e * 128 + 128)
            y = both[e][:, q * 128 : q * 128 + 128].reshape(rows, 64, 128)
            if residual is not None:
                y = y + residual[q, g0 : g0 + rows, :, lanes].astype(F32) + bias
            for n in range(rows):
                g = g0 + n
                at = (g % 2, (g + 1) // 2)
                row = y[n] * below if g >= 16 else y[n]
                f_ref[q, at[0], at[1], :, lanes] = row.astype(BF)
                if e == 1:
                    o_ref[q, n, 8:72] = row
                    f_ref[q, at[0], at[1], :, 256:384] = o_ref[q, n, 7:71].astype(BF)


def clear_shift(o_ref):
    for q in range(2):
        for n in range(o_ref.shape[1]):
            o_ref[q, n, 0:8] = jnp.zeros((8, 128), F32)


def down_conv(f_ref, kd_ref):
    rhs = jnp.concatenate([kd_ref[j, c] for j in range(3) for c in (1, 2, 0)], axis=0)
    out = []
    for q in range(2):
        lhs = jnp.concatenate(
            [
                f_ref[q, 1, 0:9].reshape(576, 384),
                f_ref[q, 0, 0:9].reshape(576, 384),
                f_ref[q, 1, 1:10].reshape(576, 384),
            ],
            axis=1,
        )
        out.append(jnp.dot(lhs, rhs, preferred_element_type=F32))
    return out


PAIR01 = ((0, 1),)
PAIR23 = ((0, 0), (1, 1))
PAIR45 = ((1, 0),)


def kernel_own(
    x_hbm, kf_hbm, ks_hbm, bf_ref, u_ref, x2_ref, w_ref, ks_ref, f45_ref, f23_ref, x_ref, kf_ref, s_ref, q_ref, o_ref, sem
):
    xs = [pltpu.make_async_copy(x_hbm.at[:, n * 4 : n * 4 + 4], x_ref.at[:, n * 4 : n * 4 + 4], sem.at[n]) for n in range(4)]
    first = pltpu.make_async_copy(kf_hbm, kf_ref, sem.at[4])
    second = pltpu.make_async_copy(ks_hbm, ks_ref, sem.at[5])
    xs[0].start()
    first.start()
    for c in xs[1:]:
        c.start()
    second.start()
    clear_edges(s_ref)
    clear_shift(o_ref)
    for k in range(4):
        for p in range(2):
            u_ref[k, p, 0] = jnp.zeros((64, 256), BF)
    for q in range(2):
        f45_ref[q, 1, 0] = jnp.zeros((64, 384), BF)
        f23_ref[q, 1, 0] = jnp.zeros((64, 384), BF)

    def row(r, carry):
        for f in range(4):
            prep_first(x_ref[f, r], f, r, u_ref, x2_ref, s_ref, q_ref)
        return carry

    for n in range(4):
        xs[n].wait()
        lax.fori_loop(n * 4, n * 4 + 4, row, 0)

    first.wait()

    def wrow(j, carry):
        zero = jnp.zeros((128, 128), BF)
        for i in range(3):
            g0, g1, g2 = (kf_ref[i, j, c] for c in range(3))
            a, b = transformed(g0.astype(F32), g1.astype(F32), g2.astype(F32))
            for k, g in enumerate((g0, a.astype(BF), b.astype(BF), g2)):
                if i == 0:
                    w_ref[k, j, 0, 0:128, 0:128] = g
                    w_ref[k, j, 0, 128:256, 128:256] = g
                    w_ref[k, j, 0, 0:128, 128:256] = zero
                    w_ref[k, j, 1, 128:256, 0:128] = zero
                elif i == 1:
                    w_ref[k, j, 0, 128:256, 0:128] = g
                    w_ref[k, j, 1, 0:128, 128:256] = g
                else:
                    w_ref[k, j, 1, 0:128, 0:128] = g
                    w_ref[k, j, 1, 128:256, 128:256] = g
        return carry

    lax.fori_loop(0, 3, wrow, 0)
    for g0, rows in ((0, 8), (8, 7)):
        first_rows(u_ref, w_ref, f45_ref, o_ref, PAIR45, g0, rows, None, None, None)
    for g0, rows in ((0, 8), (8, 7)):
        first_rows(u_ref, w_ref, f23_ref, o_ref, PAIR23, g0, rows, None, x2_ref.at[2:4], bf_ref[...])
    second.wait()


def kernel_ahead(ok_ref, u_in, x2_in, f_in, halo_ref, w_ref, kd_ref, u_ref, x2_ref, f_ref, part_ref, s_ref, q_ref, o_ref):
    clear_edges(s_ref)
    clear_shift(o_ref)
    for n in range(3):
        for f in range(4):
            prep_first(halo_ref[f, n], f, 16 + n, u_ref, x2_ref, s_ref, q_ref, n < 2)
    below = ok_ref[1].astype(F32)
    first_rows(u_ref, w_ref, f_ref, o_ref, PAIR45, 15, 3, below, None, None)
    out = down_conv(f_ref, kd_ref)
    for q in range(2):
        part_ref[q] = out[q].reshape(9, 64, 256).astype(BF)


def kernel_late(
    ok_ref, u_ref, x2_ref, f_in, w_ref, kd_ref, bf_ref, bd_ref, f_ref, red_ref, act_ref, edge_ref, o_ref
):
    clear_shift(o_ref)
    below = ok_ref[1].astype(F32)
    first_rows(u_ref, w_ref, f_ref, o_ref, PAIR23, 15, 3, below, x2_ref.at[2:4], bf_ref[...])
    out = down_conv(f_ref, kd_ref)
    for q in range(2):
        r16 = (out[q] + bd_ref[...]).astype(BF).reshape(9, 64, 256)
        red_ref[q] = r16
        act_ref[q] = silu(r16.astype(F32)).astype(BF)
        act_ref[q, 8] = (silu(r16[8].astype(F32)) * below).astype(BF)
        edge_ref[q, 0] = act_ref[q, 7]
        edge_ref[q, 1] = act_ref[q, 8]


def kernel_early(ok_ref, u_ref, x2_ref, w_ref, kd_ref, bf_ref, bd_ref, z_ref, red23_ref, red_ref, dn_ref, f_ref, o_ref):
    clear_shift(o_ref)
    below = ok_ref[1].astype(F32)
    for q in range(2):
        f_ref[q, 1, 0] = jnp.zeros((64, 384), BF)
    for g0 in (0, 9):
        first_rows(u_ref, w_ref, f_ref, o_ref, PAIR01, g0, 9, below, x2_ref.at[0:2], bf_ref[...])
    out = down_conv(f_ref, kd_ref)
    for q in range(2):
        red_ref[q] = (out[q] + bd_ref[...] + z_ref[q].reshape(576, 256).astype(F32)).astype(BF).reshape(9, 64, 256)
        for n in range(2):
            dn_ref[q, n] = red_ref[q, 7 + n]
            dn_ref[2 + q, n] = red23_ref[q, 7 + n]


def prep_mid(act, f, to, u_ref, s_ref, q_ref):
    q_ref[f, 0] = act[:, 0:128]
    q_ref[f, 1] = act[:, 128:256]
    d1 = jnp.concatenate([q_ref[f, h, pl.ds(0, 32, stride=2), :] for h in range(2)], axis=1)
    d2 = jnp.concatenate([q_ref[f, h, pl.ds(1, 32, stride=2), :] for h in range(2)], axis=1)
    s_ref[f, 0, 8:40] = d1
    s_ref[f, 1, 8:40] = d2
    d3 = s_ref[f, 0, 9:41]
    d0 = s_ref[f, 1, 7:39]
    for k, v in enumerate((d0 - d2, d1 + d2, d2 - d1, d1 - d3)):
        u_ref[(k, *to)] = v.astype(BF)


def kernel_mid(ok_ref, red01_ref, red23_ref, ks_ref, u_ref, g_ref, s_ref, q_ref):
    clear_edges(s_ref)

    def row(r, carry):
        scale = jnp.where(r == 8, ok_ref[1], 1).astype(F32)
        for f in range(4):
            v = (red01_ref, red23_ref)[f // 2][f % 2, r].astype(F32)
            prep_mid(silu(v) * scale, f, (f, r + 1), u_ref, s_ref, q_ref)
        return carry

    lax.fori_loop(1, 9, row, 0)

    def grow(i, carry):
        for j in range(3):
            a, b = transformed(*(ks_ref[i, j, c].astype(F32) for c in range(3)))
            g_ref[0, i, j] = a.astype(BF)
            g_ref[1, i, j] = b.astype(BF)
        return carry

    lax.fori_loop(0, 3, grow, 0)


def second_conv(slab, ks_ref, g_ref, red, bias, t_ref, out_ref):
    ms = []
    for k in range(4):
        lhs = jnp.concatenate([slab(k, i, j) for i in range(3) for j in range(3)], axis=1)
        if k == 0 or k == 3:
            rhs = jnp.concatenate([ks_ref[i, j, 2 * (k // 3)] for i in range(3) for j in range(3)], axis=0)
        else:
            rhs = g_ref[k - 1].reshape(2304, 256)
        ms.append(jnp.dot(lhs, rhs, preferred_element_type=F32))
    y0 = (ms[1] + ms[2] + ms[0]).reshape(16, 32, 256)
    y1 = (ms[1] - ms[2] - ms[3]).reshape(16, 32, 256)
    for n in range(16):
        for h in range(2):
            lanes = slice(h * 128, h * 128 + 128)
            t_ref[n, h, pl.ds(0, 32, stride=2), :] = y0[n, :, lanes]
            t_ref[n, h, pl.ds(1, 32, stride=2), :] = y1[n, :, lanes]
            v = t_ref[n, h] + red(n // 8, n % 8, lanes) + bias[:, lanes]
            out_ref[n // 8, n % 8, :, lanes] = v.astype(BF)


def kernel_mid_late(
    ok_ref, u_in, halo_ref, red01_ref, ks_ref, g_ref, red_ref, bs_ref, lat_ref, u_ref, s_ref, q_ref, t_ref, out_ref, sem
):
    clear_edges(s_ref)
    inner = ok_ref[0] > 0
    for f in range(4):
        own = (red01_ref, red_ref)[f // 2][f % 2, 0].astype(F32)
        above = jnp.where(inner, halo_ref[f, 1].astype(F32), own)
        prep_mid(silu(halo_ref[f, 0].astype(F32)), f, (f, 0), u_ref, s_ref, q_ref)
        prep_mid(silu(above), f, (f, 1), u_ref, s_ref, q_ref)

    def red(f, r, lanes):
        v = red_ref[f, r, :, lanes].astype(F32)
        return jnp.where(inner, halo_ref[2 + f, 1, :, lanes].astype(F32), v) if r == 0 else v

    def slab(k, i, j):
        return u_ref[k, i : i + 2, j : j + 8].reshape(512, 256)

    second_conv(slab, ks_ref, g_ref, red, bs_ref[...], t_ref, out_ref)
    copy = pltpu.make_async_copy(out_ref, lat_ref.at[2:4], sem)
    copy.start()
    copy.wait()


def kernel_mid_early(
    ok_ref, lat_in, u_ref, zact_ref, zedge_ref, halo_ref, ks_ref, g_ref, red_ref, bs_ref, lat_ref, v_ref, s_ref, q_ref, t_ref, out_ref, sem
):
    clear_edges(s_ref)
    inner = ok_ref[0] > 0

    def row(r, carry):
        for f in range(2):
            prep_mid(zact_ref[f, r].astype(F32), f, (f, r + 1), v_ref, s_ref, q_ref)
        return carry

    lax.fori_loop(1, 9, row, 0)
    for f in range(2):
        above = jnp.where(inner, zedge_ref[f, 1].astype(F32), zact_ref[f, 0].astype(F32))
        prep_mid(zedge_ref[f, 0].astype(F32), f, (f, 0), v_ref, s_ref, q_ref)
        prep_mid(above, f, (f, 1), v_ref, s_ref, q_ref)

    def red(f, r, lanes):
        v = red_ref[f, r, :, lanes].astype(F32)
        return jnp.where(inner, halo_ref[f, 1, :, lanes].astype(F32), v) if r == 0 else v

    def slab(k, i, j):
        if i == 0:
            return v_ref[k, :, j : j + 8].reshape(512, 256)
        if i == 2:
            return u_ref[k, 0:2, j : j + 8].reshape(512, 256)
        return jnp.concatenate(
            [v_ref[k, 1, j : j + 8].reshape(256, 256), u_ref[k, 0, j : j + 8].reshape(256, 256)], axis=0
        )

    second_conv(slab, ks_ref, g_ref, red, bs_ref[...], t_ref, out_ref)
    copy = pltpu.make_async_copy(out_ref, lat_ref.at[0:2], sem)
    copy.start()
    copy.wait()


V = pl.BlockSpec(memory_space=pltpu.VMEM)
ANY = pl.BlockSpec(memory_space=pl.ANY)
HBM = pl.BlockSpec(memory_space=pltpu.HBM)
SM = pl.BlockSpec(memory_space=pltpu.SMEM)


def sds(*shape):
    return jax.ShapeDtypeStruct(shape, BF)


def res(*shape):
    return VMEM(shape, BF)


def keep(*xs):
    return [pltpu.with_memory_space_constraint(x, pltpu.VMEM) for x in xs]


def call(body, name, ins, outs, scratch, flops, in_specs=None, out_specs=None, aliases=None):
    return pl.pallas_call(
        body,
        out_shape=outs,
        in_specs=in_specs or [V] * len(ins),
        out_specs=out_specs or [V] * len(outs),
        scratch_shapes=scratch,
        input_output_aliases=aliases or {},
        compiler_params=pltpu.CompilerParams(vmem_limit_bytes=LIMIT),
        cost_estimate=pl.CostEstimate(flops=flops, bytes_accessed=4 << 20, transcendentals=0),
        name=name,
    )(*ins)


def on_device(features, kf, bf, kd, bd, ks, bs):
    tm, sp = lax.axis_size("tm"), lax.axis_size("space")
    down = [(i, i + 1) for i in range(sp - 1)]
    up = [(i + 1, i) for i in range(sp - 1)]
    later = [(i, i + 1) for i in range(tm - 1)]
    cross = [(t * sp + s, (t + 1) * sp + s + 1) for t in range(tm - 1) for s in range(sp - 1)]
    at = lax.axis_index("space")
    ok = jnp.stack([(at > 0).astype(jnp.int32), (at < sp - 1).astype(jnp.int32)])
    bf2, bd2, bs2 = bf.reshape(1, 128), bd.reshape(1, 256), bs.reshape(1, 256)

    halo = lax.ppermute(features[:, 0:3], "space", up)
    wide = [VMEM((4, 2, 80, 128), F32), VMEM((4, 128, 128), F32)]
    shift = lambda n: VMEM((2, n, 72, 128), F32)
    fshape = (2, 2, 10, 64, 384)
    u, x2, w, ksv, f45, f23 = call(
        kernel_own, "own", (*[pltpu.with_memory_space_constraint(v, pltpu.HBM) for v in (features, kf, ks)], bf2),
        [res(4, 2, 20, 64, 256), res(4, 18, 64, 256), res(4, 3, 2, 256, 256), res(3, 3, 3, 256, 256), res(*fshape), res(*fshape)],
        [VMEM((4, 16, 128, 128), BF), VMEM((3, 3, 3, 128, 128), BF), *wide, shift(8), pltpu.SemaphoreType.DMA((6,))],
        6_000_000_000, in_specs=[HBM, HBM, HBM, V],
    )
    u, x2, _, part = call(
        kernel_ahead, "ahead", (ok, *keep(u, x2, f45), halo, *keep(w), kd),
        [res(4, 2, 20, 64, 256), res(4, 18, 64, 256), res(*fshape), sds(2, 9, 64, 256)],
        [*wide, shift(3)], 2_000_000_000, in_specs=[SM] + [V] * 6, aliases={1: 0, 2: 1, 3: 2},
    )
    zpart = lax.ppermute(part, "tm", later)
    _, red23, act23, edge23 = call(
        kernel_late, "late", (ok, *keep(u, x2, f23, w), kd, bf2, bd2),
        [res(*fshape), res(2, 9, 64, 256), sds(2, 9, 64, 256), sds(2, 2, 64, 256)],
        [shift(3)], 2_500_000_000, in_specs=[SM] + [V] * 7, aliases={3: 0},
    )
    zact = lax.ppermute(act23, "tm", later)
    zedge = lax.ppermute(edge23, ("tm", "space"), cross)
    red01, dn = call(
        kernel_early, "early", (ok, *keep(u, x2, w), kd, bf2, bd2, zpart, *keep(red23)),
        [res(2, 9, 64, 256), sds(4, 2, 64, 256)],
        [VMEM(fshape, BF), shift(9)], 3_000_000_000, in_specs=[SM] + [V] * 8,
    )
    halo_mid = lax.ppermute(dn, "space", down)
    half = lambda n: [VMEM((n, 2, 48, 256), F32), VMEM((n, 2, 64, 128), F32)]
    tail = [VMEM((16, 2, 64, 128), F32), VMEM((2, 8, 64, 256), BF), pltpu.SemaphoreType.DMA]
    u2, g = call(
        kernel_mid, "mid", (ok, *keep(red01, red23, ksv)),
        [res(4, 4, 10, 32, 256), res(2, 3, 3, 256, 256)], half(4), 1_500_000_000, in_specs=[SM] + [V] * 3,
    )
    lat, u2 = call(
        kernel_mid_late, "mid_late", (ok, *keep(u2), halo_mid, *keep(red01, ksv, g, red23), bs2),
        [sds(4, 8, 64, 256), res(4, 4, 10, 32, 256)],
        half(4) + tail, 3_000_000_000, in_specs=[SM] + [V] * 7, out_specs=[ANY, V], aliases={1: 1},
    )
    (lat,) = call(
        kernel_mid_early, "mid_early", (ok, lat, *keep(u2), zact, zedge, halo_mid, *keep(ksv, g, red01), bs2),
        [sds(4, 8, 64, 256)],
        [VMEM((4, 2, 10, 32, 256), BF)] + half(2) + tail,
        3_000_000_000, in_specs=[SM, ANY] + [V] * 8, out_specs=[ANY], aliases={1: 0},
    )
    return lat


def solution(mesh):
    in_specs = (P("tm", "space", None, None), P(), P(), P(), P(), P(), P())
    out_specs = P("tm", "space", None, None)
    return jax.shard_map(on_device, mesh=mesh, in_specs=in_specs, out_specs=out_specs, check_vma=False)
```

```python
import jax
import jax.numpy as jnp
from jax import lax
from jax.experimental import pallas as pl
from jax.experimental.pallas import tpu as pltpu
from jax.sharding import PartitionSpec as P

BF = jnp.bfloat16
F32 = jnp.float32
VMEM = pltpu.VMEM
LIMIT = 24 * 2**20


def silu(v):
    h = 0.5 * v
    return h + h * jnp.tanh(h)


def clear_edges(s_ref):
    for f in range(s_ref.shape[0]):
        for e in range(2):
            s_ref[f, e, 0:8] = jnp.zeros((8, s_ref.shape[-1]), F32)
            s_ref[f, e, s_ref.shape[2] - 8 :] = jnp.zeros((8, s_ref.shape[-1]), F32)


def prep_first(x, f, r, u_ref, x2_ref, s_ref, q_ref, residual=True):
    q_ref[f] = x.astype(F32)
    even = q_ref[f, pl.ds(0, 64, stride=2), :]
    odd = q_ref[f, pl.ds(1, 64, stride=2), :]
    d1 = silu(even)
    d2 = silu(odd)
    s_ref[f, 0, 8:72] = d1
    s_ref[f, 1, 8:72] = d2
    d3 = s_ref[f, 0, 9:73]
    d0 = s_ref[f, 1, 7:71]
    lanes = slice((f % 2) * 128, (f % 2) * 128 + 128)
    for k, v in enumerate((d0 - d2, d1 + d2, d2 - d1, d1 - d3)):
        u_ref[k, f // 2, r + 1, :, lanes] = v.astype(BF)
    if residual:
        x2_ref[f, r, :, 0:128] = even.astype(BF)
        x2_ref[f, r, :, 128:256] = odd.astype(BF)


def transformed(g0, g1, g2):
    half = 0.5 * (g0 + g2)
    return half + 0.5 * g1, half - 0.5 * g1


class Pump:
    def __init__(self, work, slots):
        self.work, self.slots = list(work), slots

    def __call__(self):
        count = -(-len(self.work) // max(self.slots, 1))
        self.slots -= 1
        for _ in range(count):
            self.work.pop(0)()


def idle():
    pass


def first_rows(u_ref, w_ref, f_ref, o_ref, pairs, g0, rows, below, residual, bias, pump=idle):
    ms = []
    for k in range(4):
        lhs = jnp.concatenate(
            [u_ref[k, p, g0 + j : g0 + j + rows].reshape(rows * 64, 256) for j in range(3) for p, _ in pairs], axis=1
        )
        rhs = jnp.concatenate([w_ref[k, j, which] for j in range(3) for _, which in pairs], axis=0)
        ms.append(jnp.dot(lhs, rhs, preferred_element_type=F32))
        pump()
    both = (ms[1] + ms[2] + ms[0], ms[1] - ms[2] - ms[3])
    for q in range(2):
        for e in range(2):
            lanes = slice(e * 128, e * 128 + 128)
            y = both[e][:, q * 128 : q * 128 + 128].reshape(rows, 64, 128)
            if residual is not None:
                y = y + residual[q, g0 : g0 + rows, :, lanes].astype(F32) + bias
            for n in range(rows):
                g = g0 + n
                at = (g % 2, (g + 1) // 2)
                row = y[n] * below if g >= 16 else y[n]
                f_ref[q, at[0], at[1], :, lanes] = row.astype(BF)
                if e == 1:
                    o_ref[q, n, 8:72] = row
                    f_ref[q, at[0], at[1], :, 256:384] = o_ref[q, n, 7:71].astype(BF)


def clear_shift(o_ref):
    for q in range(2):
        for n in range(o_ref.shape[1]):
            o_ref[q, n, 0:8] = jnp.zeros((8, 128), F32)


def down_conv(f_ref, kd_ref):
    rhs = jnp.concatenate([kd_ref[j, c] for j in range(3) for c in (1, 2, 0)], axis=0)
    out = []
    for q in range(2):
        lhs = jnp.concatenate(
            [
                f_ref[q, 1, 0:9].reshape(576, 384),
                f_ref[q, 0, 0:9].reshape(576, 384),
                f_ref[q, 1, 1:10].reshape(576, 384),
            ],
            axis=1,
        )
        out.append(jnp.dot(lhs, rhs, preferred_element_type=F32))
    return out


PAIR01 = ((0, 1),)
PAIR23 = ((0, 0), (1, 1))
PAIR45 = ((1, 0),)


def kernel_own(
    x_hbm, kf_hbm, ks_hbm, kd_hbm, bf_hbm, bd_hbm, bs_hbm,
    u_ref, x2_ref, w_ref, ks_ref, kd_ref, bf_ref, bd_ref, bs_ref, f45_ref, f23_ref,
    x_ref, kf_ref, s_ref, q_ref, o_ref, sem,
):
    xs = [pltpu.make_async_copy(x_hbm.at[:, n * 4 : n * 4 + 4], x_ref.at[:, n * 4 : n * 4 + 4], sem.at[n]) for n in range(4)]
    first = pltpu.make_async_copy(kf_hbm, kf_ref, sem.at[4])
    pairs = ((ks_hbm, ks_ref), (kd_hbm, kd_ref), (bf_hbm, bf_ref), (bd_hbm, bd_ref), (bs_hbm, bs_ref))
    rest = [pltpu.make_async_copy(a, b, sem.at[5 + n]) for n, (a, b) in enumerate(pairs)]
    xs[0].start()
    xs[1].start()
    first.start()
    rest[2].start()
    xs[2].start()
    xs[3].start()
    for n in (0, 1, 3, 4):
        rest[n].start()
    clear_edges(s_ref)
    clear_shift(o_ref)
    for k in range(4):
        for p in range(2):
            u_ref[k, p, 0] = jnp.zeros((64, 256), BF)
    for q in range(2):
        f45_ref[q, 1, 0] = jnp.zeros((64, 384), BF)
        f23_ref[q, 1, 0] = jnp.zeros((64, 384), BF)

    def row(r, carry):
        for f in range(4):
            prep_first(x_ref[f, r], f, r, u_ref, x2_ref, s_ref, q_ref)
        return carry

    for n in range(2):
        xs[n].wait()
        lax.fori_loop(n * 4, n * 4 + 4, row, 0)

    first.wait()

    def wrow(j, carry):
        zero = jnp.zeros((128, 128), BF)
        for i in range(3):
            g0, g1, g2 = (kf_ref[i, j, c] for c in range(3))
            a, b = transformed(g0.astype(F32), g1.astype(F32), g2.astype(F32))
            for k, g in enumerate((g0, a.astype(BF), b.astype(BF), g2)):
                if i == 0:
                    w_ref[k, j, 0, 0:128, 0:128] = g
                    w_ref[k, j, 0, 128:256, 128:256] = g
                    w_ref[k, j, 0, 0:128, 128:256] = zero
                    w_ref[k, j, 1, 128:256, 0:128] = zero
                elif i == 1:
                    w_ref[k, j, 0, 128:256, 0:128] = g
                    w_ref[k, j, 1, 0:128, 128:256] = g
                else:
                    w_ref[k, j, 1, 0:128, 0:128] = g
                    w_ref[k, j, 1, 128:256, 128:256] = g
        return carry

    lax.fori_loop(0, 3, wrow, 0)
    rest[2].wait()
    xs[2].wait()
    xs[3].wait()
    pump = Pump(
        [
            lambda f=f, r=r: prep_first(x_ref[f, r], f, r, u_ref, x2_ref, s_ref, q_ref)
            for r in range(8, 16)
            for f in range(4)
        ],
        8,
    )
    first_rows(u_ref, w_ref, f45_ref, o_ref, PAIR45, 0, 7, None, None, None, pump)
    first_rows(u_ref, w_ref, f23_ref, o_ref, PAIR23, 0, 7, None, x2_ref.at[2:4], bf_ref[...], pump)
    first_rows(u_ref, w_ref, f45_ref, o_ref, PAIR45, 7, 8, None, None, None)
    first_rows(u_ref, w_ref, f23_ref, o_ref, PAIR23, 7, 8, None, x2_ref.at[2:4], bf_ref[...])
    for n in (0, 1, 3, 4):
        rest[n].wait()


def kernel_ahead(ok_ref, u_in, x2_in, f_in, halo_ref, w_ref, kd_ref, u_ref, x2_ref, f_ref, part_ref, s_ref, q_ref, o_ref):
    clear_edges(s_ref)
    clear_shift(o_ref)
    for n in range(3):
        for f in range(4):
            prep_first(halo_ref[f, n], f, 16 + n, u_ref, x2_ref, s_ref, q_ref, n < 2)
    below = ok_ref[1].astype(F32)
    first_rows(u_ref, w_ref, f_ref, o_ref, PAIR45, 15, 3, below, None, None)
    out = down_conv(f_ref, kd_ref)
    for q in range(2):
        part_ref[q] = out[q].reshape(9, 64, 256).astype(BF)


def kernel_late(ok_ref, u_ref, x2_ref, f_in, w_ref, kd_ref, bf_ref, bd_ref, f_ref, red_ref, o_ref):
    clear_shift(o_ref)
    below = ok_ref[1].astype(F32)
    first_rows(u_ref, w_ref, f_ref, o_ref, PAIR23, 15, 3, below, x2_ref.at[2:4], bf_ref[...])
    out = down_conv(f_ref, kd_ref)
    for q in range(2):
        red_ref[q] = (out[q] + bd_ref[...]).astype(BF).reshape(9, 64, 256)


def prep_mid(act, f, to, u_ref, s_ref, q_ref):
    q_ref[f, 0] = act[:, 0:128]
    q_ref[f, 1] = act[:, 128:256]
    d1 = jnp.concatenate([q_ref[f, h, pl.ds(0, 32, stride=2), :] for h in range(2)], axis=1)
    d2 = jnp.concatenate([q_ref[f, h, pl.ds(1, 32, stride=2), :] for h in range(2)], axis=1)
    s_ref[f, 0, 8:40] = d1
    s_ref[f, 1, 8:40] = d2
    d3 = s_ref[f, 0, 9:41]
    d0 = s_ref[f, 1, 7:39]
    for k, v in enumerate((d0 - d2, d1 + d2, d2 - d1, d1 - d3)):
        u_ref[(k, *to)] = v.astype(BF)


def own_row(ok_ref, red_ref, f, r, u_ref, s_ref, q_ref):
    act = silu(red_ref[f % 2, r].astype(F32))
    if r == 8:
        act = act * ok_ref[1].astype(F32)
    prep_mid(act, f, (f, r + 1), u_ref, s_ref, q_ref)


def kernel_early(
    ok_ref, u_ref, x2_ref, w_ref, kd_ref, bf_ref, bd_ref, ks_ref, red_ref, p_ref, u2_ref, g_ref, f_ref, o_ref, s_ref, q_ref
):
    clear_shift(o_ref)
    clear_edges(s_ref)
    below = ok_ref[1].astype(F32)
    for q in range(2):
        f_ref[q, 1, 0] = jnp.zeros((64, 384), BF)

    def weights(i, j):
        a, b = transformed(*(ks_ref[i, j, c].astype(F32) for c in range(3)))
        g_ref[0, i, j] = a.astype(BF)
        g_ref[1, i, j] = b.astype(BF)

    work = [lambda f=f, r=r: own_row(ok_ref, red_ref, f, r, u2_ref, s_ref, q_ref) for r in range(1, 9) for f in (2, 3)]
    work += [lambda i=i, j=j: weights(i, j) for i in range(3) for j in range(3)]
    pump = Pump(work, 8)
    for g0 in (0, 9):
        first_rows(u_ref, w_ref, f_ref, o_ref, PAIR01, g0, 9, below, x2_ref.at[0:2], bf_ref[...], pump)
    out = down_conv(f_ref, kd_ref)
    for q in range(2):
        p_ref[q] = (out[q] + bd_ref[...]).reshape(9, 64, 256)


def kernel_join(p_ref, z_ref, red23_ref, red_ref, dn_ref):
    for q in range(2):
        for r in range(9):
            red_ref[q, r] = (p_ref[q, r] + z_ref[q, r].astype(F32)).astype(BF)
        for n in range(2):
            dn_ref[q, n] = red_ref[q, 7 + n]
            dn_ref[2 + q, n] = red23_ref[q, 7 + n]


def taps(ks_ref, g_ref, k, i):
    if k == 0 or k == 3:
        return jnp.concatenate([ks_ref[i, j, 2 * (k // 3)] for j in range(3)], axis=0)
    return g_ref[k - 1, i].reshape(768, 256)


def columns(t_ref, at, y0, y1):
    for h in range(2):
        lanes = slice(h * 128, h * 128 + 128)
        t_ref[(*at, h, pl.ds(0, 32, stride=2), slice(None))] = y0[:, lanes]
        t_ref[(*at, h, pl.ds(1, 32, stride=2), slice(None))] = y1[:, lanes]


def outer_pairs(u_ref, ks_ref, g_ref, r0, rows, zl_ref, y_ref, t_ref, pump=idle):
    n = rows * 32

    def lhs(k, a, b):
        return jnp.concatenate(
            [
                jnp.concatenate([u_ref[k, f, r0 + j : r0 + j + rows].reshape(n, 256) for f in (a, b)], axis=0)
                for j in range(3)
            ],
            axis=1,
        )

    first, later, own = [], [], []
    for k in range(4):
        first.append(jnp.dot(lhs(k, 2, 3), taps(ks_ref, g_ref, k, 0), preferred_element_type=F32))
        pump()
    for k in range(4):
        d1 = jnp.dot(lhs(k, 3, 0), taps(ks_ref, g_ref, k, 1), preferred_element_type=F32)
        d2 = jnp.dot(lhs(k, 0, 1), taps(ks_ref, g_ref, k, 2), preferred_element_type=F32)
        later.append((first[k][:n] + d1[:n], first[k][n:]))
        own.append((d2[:n], d2[n:] + d1[n:]))
    for f in range(2):
        for ms, to in ((later, t_ref), (own, y_ref)):
            y0 = (ms[1][f] + ms[2][f] + ms[0][f]).reshape(rows, 32, 256)
            y1 = (ms[1][f] - ms[2][f] - ms[3][f]).reshape(rows, 32, 256)
            for r in range(rows):
                columns(to, (f, r0 + r), y0[r], y1[r])
        for r in range(r0, r0 + rows):
            for h in range(2):
                zl_ref[f, r, :, h * 128 : h * 128 + 128] = t_ref[f, r, h].astype(BF)


def kernel_inner(ok_ref, u_in, red01_ref, ks_ref, g_ref, u_ref, zl_ref, y_ref, s_ref, q_ref, t_ref):
    clear_edges(s_ref)
    work = [lambda f=f, r=r: own_row(ok_ref, red01_ref, f, r, u_ref, s_ref, q_ref) for r in range(1, 9) for f in (0, 1)]
    outer_pairs(u_ref, ks_ref, g_ref, 2, 6, zl_ref, y_ref, t_ref, Pump(work, 4))


def kernel_edge(
    ok_ref, u_in, zl_in, y_in, halo_ref, red01_ref, red23_ref, ks_ref, g_ref, u_ref, zl_ref, y_ref, s_ref, q_ref, t_ref
):
    clear_edges(s_ref)
    inner = ok_ref[0] > 0
    for f in range(4):
        own = (red01_ref, red23_ref)[f // 2][f % 2, 0].astype(F32)
        above = jnp.where(inner, halo_ref[f, 1].astype(F32), own)
        prep_mid(silu(halo_ref[f, 0].astype(F32)), f, (f, 0), u_ref, s_ref, q_ref)
        prep_mid(silu(above), f, (f, 1), u_ref, s_ref, q_ref)
    outer_pairs(u_ref, ks_ref, g_ref, 0, 2, zl_ref, y_ref, t_ref)


def kernel_mid_late(ok_ref, u_ref, halo_ref, ks_ref, g_ref, red_ref, bs_ref, out_ref, t_ref):
    inner = ok_ref[0] > 0
    ms = []
    for k in range(4):
        lhs = jnp.concatenate(
            [u_ref[k, i : i + 2, j : j + 8].reshape(512, 256) for i in range(3) for j in range(3)], axis=1
        )
        rhs = jnp.concatenate([taps(ks_ref, g_ref, k, i) for i in range(3)], axis=0)
        ms.append(jnp.dot(lhs, rhs, preferred_element_type=F32))
    y0 = (ms[1] + ms[2] + ms[0]).reshape(2, 8, 32, 256)
    y1 = (ms[1] - ms[2] - ms[3]).reshape(2, 8, 32, 256)
    for f in range(2):
        for r in range(8):
            columns(t_ref, (f, r), y0[f, r], y1[f, r])
            for h in range(2):
                lanes = slice(h * 128, h * 128 + 128)
                v = red_ref[f, r, :, lanes].astype(F32)
                if r == 0:
                    v = jnp.where(inner, halo_ref[2 + f, 1, :, lanes].astype(F32), v)
                out_ref[f, r, :, lanes] = (t_ref[f, r, h] + v + bs_ref[:, lanes]).astype(BF)


def kernel_last(ok_ref, late_ref, y_ref, zl_ref, halo_ref, red_ref, bs_ref, lat_ref, out_ref, sem):
    inner = ok_ref[0] > 0
    copies = [pltpu.make_async_copy(late_ref, lat_ref.at[2:4], sem.at[0])]
    copies[0].start()
    for f in range(2):
        for r in range(8):
            for h in range(2):
                lanes = slice(h * 128, h * 128 + 128)
                v = red_ref[f, r, :, lanes].astype(F32)
                if r == 0:
                    v = jnp.where(inner, halo_ref[f, 1, :, lanes].astype(F32), v)
                v = v + zl_ref[f, r, :, lanes].astype(F32) + bs_ref[:, lanes]
                out_ref[f, r, :, lanes] = (y_ref[f, r, h] + v).astype(BF)
        copies.append(pltpu.make_async_copy(out_ref.at[f], lat_ref.at[f], sem.at[1 + f]))
        copies[-1].start()
    for c in copies:
        c.wait()


V = pl.BlockSpec(memory_space=pltpu.VMEM)
ANY = pl.BlockSpec(memory_space=pl.ANY)
HBM = pl.BlockSpec(memory_space=pltpu.HBM)
SM = pl.BlockSpec(memory_space=pltpu.SMEM)


def sds(*shape):
    return jax.ShapeDtypeStruct(shape, BF)


def res(*shape, dtype=BF):
    return VMEM(shape, dtype)


def keep(*xs):
    return [pltpu.with_memory_space_constraint(x, pltpu.VMEM) for x in xs]


def far(*xs):
    return [pltpu.with_memory_space_constraint(x, pltpu.HBM) for x in xs]


def call(body, name, ins, outs, scratch, flops, in_specs=None, out_specs=None, aliases=None):
    return pl.pallas_call(
        body,
        out_shape=outs,
        in_specs=in_specs or [V] * len(ins),
        out_specs=out_specs or [V] * len(outs),
        scratch_shapes=scratch,
        input_output_aliases=aliases or {},
        compiler_params=pltpu.CompilerParams(vmem_limit_bytes=LIMIT),
        cost_estimate=pl.CostEstimate(flops=flops, bytes_accessed=4 << 20, transcendentals=0),
        name=name,
    )(*ins)


def on_device(features, kf, bf, kd, bd, ks, bs):
    tm, sp = lax.axis_size("tm"), lax.axis_size("space")
    down = [(i, i + 1) for i in range(sp - 1)]
    up = [(i + 1, i) for i in range(sp - 1)]
    later = [(i, i + 1) for i in range(tm - 1)]
    at = lax.axis_index("space")
    ok = jnp.stack([(at > 0).astype(jnp.int32), (at < sp - 1).astype(jnp.int32)])

    halo = lax.ppermute(features[:, 0:3], "space", up)
    wide = [VMEM((4, 2, 80, 128), F32), VMEM((4, 128, 128), F32)]
    half = [VMEM((4, 2, 48, 256), F32), VMEM((4, 2, 64, 128), F32)]
    shift = lambda n: VMEM((2, n, 72, 128), F32)
    fshape, ushape, u2shape = (2, 2, 10, 64, 384), (4, 2, 20, 64, 256), (4, 4, 10, 32, 256)
    yshape = (2, 8, 2, 64, 128)
    u, x2, w, ksv, kdv, bfv, bdv, bsv, f45, f23 = call(
        kernel_own, "own", far(features, kf, ks, kd, bf.reshape(1, 128), bd.reshape(1, 256), bs.reshape(1, 256)),
        [
            res(*ushape), res(4, 18, 64, 256), res(4, 3, 2, 256, 256), res(3, 3, 3, 256, 256), res(3, 3, 128, 256),
            res(1, 128, dtype=F32), res(1, 256, dtype=F32), res(1, 256, dtype=F32), res(*fshape), res(*fshape),
        ],
        [VMEM((4, 16, 128, 128), BF), VMEM((3, 3, 3, 128, 128), BF), *wide, shift(8), pltpu.SemaphoreType.DMA((10,))],
        6_000_000_000, in_specs=[HBM] * 7,
    )
    u, x2, _, part = call(
        kernel_ahead, "ahead", (ok, *keep(u, x2, f45), halo, *keep(w, kdv)),
        [res(*ushape), res(4, 18, 64, 256), res(*fshape), sds(2, 9, 64, 256)],
        [*wide, shift(3)], 2_000_000_000, in_specs=[SM] + [V] * 6, aliases={1: 0, 2: 1, 3: 2},
    )
    zpart = lax.ppermute(part, "tm", later)
    _, red23 = call(
        kernel_late, "late", (ok, *keep(u, x2, f23, w, kdv, bfv, bdv)),
        [res(*fshape), res(2, 9, 64, 256)],
        [shift(3)], 2_500_000_000, in_specs=[SM] + [V] * 7, aliases={3: 0},
    )
    p01, u2, g = call(
        kernel_early, "early", (ok, *keep(u, x2, w, kdv, bfv, bdv, ksv, red23)),
        [res(2, 9, 64, 256, dtype=F32), res(*u2shape), res(2, 3, 3, 256, 256)],
        [VMEM(fshape, BF), shift(9), *half], 3_000_000_000, in_specs=[SM] + [V] * 8,
    )
    red01, dn = call(
        kernel_join, "join", (*keep(p01), zpart, *keep(red23)), [res(2, 9, 64, 256), sds(4, 2, 64, 256)], [], 500_000_000
    )
    halo_mid = lax.ppermute(dn, "space", down)
    u2, zl, y = call(
        kernel_inner, "inner", (ok, *keep(u2, red01, ksv, g)),
        [res(*u2shape), res(2, 8, 64, 256), res(*yshape, dtype=F32)],
        [*half, VMEM(yshape, F32)], 3_000_000_000, in_specs=[SM] + [V] * 4, aliases={1: 0},
    )
    u2, zl, y = call(
        kernel_edge, "edge", (ok, *keep(u2, zl, y), halo_mid, *keep(red01, red23, ksv, g)),
        [res(*u2shape), res(2, 8, 64, 256), res(*yshape, dtype=F32)],
        [*half, VMEM(yshape, F32)], 1_500_000_000, in_specs=[SM] + [V] * 8, aliases={1: 0, 2: 1, 3: 2},
    )
    zlat = lax.ppermute(zl, "tm", later)
    late = call(
        kernel_mid_late, "mid_late", (ok, *keep(u2), halo_mid, *keep(ksv, g, red23, bsv)),
        [res(2, 8, 64, 256)], [VMEM(yshape, F32)], 4_000_000_000, in_specs=[SM] + [V] * 6,
    )
    (lat,) = call(
        kernel_last, "last", (ok, *keep(late[0], y), zlat, halo_mid, *keep(red01, bsv)),
        [sds(4, 8, 64, 256)], [VMEM((2, 8, 64, 256), BF), pltpu.SemaphoreType.DMA((3,))],
        500_000_000, in_specs=[SM] + [V] * 6, out_specs=[HBM],
    )
    return lat


def solution(mesh):
    in_specs = (P("tm", "space", None, None), P(), P(), P(), P(), P(), P())
    out_specs = P("tm", "space", None, None)
    return jax.shard_map(on_device, mesh=mesh, in_specs=in_specs, out_specs=out_specs, check_vma=False)
```

```python
import jax
import jax.numpy as jnp
from jax import lax
from jax.experimental import pallas as pl
from jax.experimental.pallas import tpu as pltpu
from jax.sharding import PartitionSpec as P

BF = jnp.bfloat16
F32 = jnp.float32
VMEM = pltpu.VMEM
LIMIT = 24 * 2**20
STEP = 4


def silu(v):
    h = 0.5 * v
    return h + h * jnp.tanh(h)


def clear_edges(s_ref):
    for f in range(s_ref.shape[0]):
        for e in range(2):
            s_ref[f, e, 0:8] = jnp.zeros((8, s_ref.shape[-1]), F32)
            s_ref[f, e, s_ref.shape[2] - 8 :] = jnp.zeros((8, s_ref.shape[-1]), F32)


def prep_first(x, f, r, u_ref, x2_ref, s_ref, q_ref, residual=True):
    q_ref[f] = x.astype(F32)
    even = q_ref[f, pl.ds(0, 64, stride=2), :]
    odd = q_ref[f, pl.ds(1, 64, stride=2), :]
    d1 = silu(even)
    d2 = silu(odd)
    s_ref[f, 0, 8:72] = d1
    s_ref[f, 1, 8:72] = d2
    d3 = s_ref[f, 0, 9:73]
    d0 = s_ref[f, 1, 7:71]
    lanes = slice((f % 2) * 128, (f % 2) * 128 + 128)
    for k, v in enumerate((d0 - d2, d1 + d2, d2 - d1, d1 - d3)):
        u_ref[k, f // 2, r + 1, :, lanes] = v.astype(BF)
    if residual:
        x2_ref[f, r, :, 0:128] = even.astype(BF)
        x2_ref[f, r, :, 128:256] = odd.astype(BF)


def transformed(g0, g1, g2):
    half = 0.5 * (g0 + g2)
    return half + 0.5 * g1, half - 0.5 * g1


class Pump:
    def __init__(self, work, slots):
        self.work, self.slots = list(work), slots

    def __call__(self):
        count = -(-len(self.work) // max(self.slots, 1))
        self.slots -= 1
        for _ in range(count):
            self.work.pop(0)()


def idle():
    pass


def first_rows(u_ref, w_ref, f_ref, o_ref, pairs, g0, rows, below, residual, bias, pump=idle):
    ms = []
    for k in range(4):
        lhs = jnp.concatenate(
            [u_ref[k, p, g0 + j : g0 + j + rows].reshape(rows * 64, 256) for j in range(3) for p, _ in pairs], axis=1
        )
        rhs = jnp.concatenate([w_ref[k, j, which] for j in range(3) for _, which in pairs], axis=0)
        ms.append(jnp.dot(lhs, rhs, preferred_element_type=F32))
        pump()
    both = (ms[1] + ms[2] + ms[0], ms[1] - ms[2] - ms[3])
    for q in range(2):
        for e in range(2):
            lanes = slice(e * 128, e * 128 + 128)
            y = both[e][:, q * 128 : q * 128 + 128].reshape(rows, 64, 128)
            if residual is not None:
                y = y + residual[q, g0 : g0 + rows, :, lanes].astype(F32) + bias
            for n in range(rows):
                g = g0 + n
                at = (g % 2, (g + 1) // 2)
                row = y[n] * below if g >= 16 else y[n]
                f_ref[q, at[0], at[1], :, lanes] = row.astype(BF)
                if e == 1:
                    o_ref[q, n, 8:72] = row
                    f_ref[q, at[0], at[1], :, 256:384] = o_ref[q, n, 7:71].astype(BF)


def clear_shift(o_ref):
    for q in range(2):
        for n in range(o_ref.shape[1]):
            o_ref[q, n, 0:8] = jnp.zeros((8, 128), F32)


def down_conv(f_ref, kd_ref, pump=idle):
    rhs = jnp.concatenate([kd_ref[j, c] for j in range(3) for c in (1, 2, 0)], axis=0)
    out = []
    for q in range(2):
        lhs = jnp.concatenate(
            [
                f_ref[q, 1, 0:9].reshape(576, 384),
                f_ref[q, 0, 0:9].reshape(576, 384),
                f_ref[q, 1, 1:10].reshape(576, 384),
            ],
            axis=1,
        )
        out.append(jnp.dot(lhs, rhs, preferred_element_type=F32))
        pump()
    return out


PAIR01 = ((0, 1),)
PAIR23 = ((0, 0), (1, 1))
PAIR45 = ((1, 0),)


def kernel_own(
    x_hbm, kf_hbm, ks_hbm, kd_hbm, bf_hbm, bd_hbm, bs_hbm,
    u_ref, x2_ref, w_ref, ks_ref, kd_ref, bf_ref, bd_ref, bs_ref, f45_ref, f23_ref, f01_ref,
    x_ref, kf_ref, s_ref, q_ref, o_ref, sem,
):
    xs = [pltpu.make_async_copy(x_hbm.at[:, n * 4 : n * 4 + 4], x_ref.at[:, n * 4 : n * 4 + 4], sem.at[n]) for n in range(4)]
    first = pltpu.make_async_copy(kf_hbm, kf_ref, sem.at[4])
    pairs = ((ks_hbm, ks_ref), (kd_hbm, kd_ref), (bf_hbm, bf_ref), (bd_hbm, bd_ref), (bs_hbm, bs_ref))
    rest = [pltpu.make_async_copy(a, b, sem.at[5 + n]) for n, (a, b) in enumerate(pairs)]
    xs[0].start()
    xs[1].start()
    first.start()
    rest[2].start()
    xs[2].start()
    xs[3].start()
    for n in (0, 1, 3, 4):
        rest[n].start()
    clear_edges(s_ref)
    clear_shift(o_ref)
    for k in range(4):
        for p in range(2):
            u_ref[k, p, 0] = jnp.zeros((64, 256), BF)
    for q in range(2):
        f45_ref[q, 1, 0] = jnp.zeros((64, 384), BF)
        f23_ref[q, 1, 0] = jnp.zeros((64, 384), BF)
        f01_ref[q, 1, 0] = jnp.zeros((64, 384), BF)

    def row(r, carry):
        for f in range(4):
            prep_first(x_ref[f, r], f, r, u_ref, x2_ref, s_ref, q_ref)
        return carry

    for n in range(2):
        xs[n].wait()
        lax.fori_loop(n * 4, n * 4 + 4, row, 0)

    first.wait()

    def wrow(j, carry):
        zero = jnp.zeros((128, 128), BF)
        for i in range(3):
            g0, g1, g2 = (kf_ref[i, j, c] for c in range(3))
            a, b = transformed(g0.astype(F32), g1.astype(F32), g2.astype(F32))
            for k, g in enumerate((g0, a.astype(BF), b.astype(BF), g2)):
                if i == 0:
                    w_ref[k, j, 0, 0:128, 0:128] = g
                    w_ref[k, j, 0, 128:256, 128:256] = g
                    w_ref[k, j, 0, 0:128, 128:256] = zero
                    w_ref[k, j, 1, 128:256, 0:128] = zero
                elif i == 1:
                    w_ref[k, j, 0, 128:256, 0:128] = g
                    w_ref[k, j, 1, 0:128, 128:256] = g
                else:
                    w_ref[k, j, 1, 0:128, 0:128] = g
                    w_ref[k, j, 1, 128:256, 128:256] = g
        return carry

    lax.fori_loop(0, 3, wrow, 0)
    rest[2].wait()
    xs[2].wait()
    xs[3].wait()
    pump = Pump(
        [
            lambda f=f, r=r: prep_first(x_ref[f, r], f, r, u_ref, x2_ref, s_ref, q_ref)
            for r in range(8, 16)
            for f in range(4)
        ],
        12,
    )
    for g0, rows, p in ((0, 7, pump), (7, 8, idle)):
        first_rows(u_ref, w_ref, f45_ref, o_ref, PAIR45, g0, rows, None, None, None, p)
        first_rows(u_ref, w_ref, f23_ref, o_ref, PAIR23, g0, rows, None, x2_ref.at[2:4], bf_ref[...], p)
        first_rows(u_ref, w_ref, f01_ref, o_ref, PAIR01, g0, rows, None, x2_ref.at[0:2], bf_ref[...], p)
    for n in (0, 1, 3, 4):
        rest[n].wait()


def kernel_ahead(ok_ref, u_in, x2_in, f_in, halo_ref, w_ref, kd_ref, u_ref, x2_ref, f_ref, part_ref, s_ref, q_ref, o_ref):
    clear_edges(s_ref)
    clear_shift(o_ref)
    for n in range(3):
        for f in range(4):
            prep_first(halo_ref[f, n], f, 16 + n, u_ref, x2_ref, s_ref, q_ref, n < 2)
    below = ok_ref[1].astype(F32)
    first_rows(u_ref, w_ref, f_ref, o_ref, PAIR45, 15, 3, below, None, None)
    out = down_conv(f_ref, kd_ref)
    for q in range(2):
        part_ref[q] = out[q].reshape(9, 64, 256).astype(BF)


def kernel_late(ok_ref, u_ref, x2_ref, f_in, w_ref, kd_ref, bf_ref, bd_ref, f_ref, red_ref, dn_ref, o_ref):
    clear_shift(o_ref)
    below = ok_ref[1].astype(F32)
    first_rows(u_ref, w_ref, f_ref, o_ref, PAIR23, 15, 3, below, x2_ref.at[2:4], bf_ref[...])
    out = down_conv(f_ref, kd_ref)
    for q in range(2):
        red_ref[q] = (out[q] + bd_ref[...]).astype(BF).reshape(9, 64, 256)
        for n in range(2):
            dn_ref[q, n] = red_ref[q, 7 + n]


def prep_mid(act, f, to, u_ref, s_ref, q_ref):
    q_ref[f, 0] = act[:, 0:128]
    q_ref[f, 1] = act[:, 128:256]
    d1 = jnp.concatenate([q_ref[f, h, pl.ds(0, 32, stride=2), :] for h in range(2)], axis=1)
    d2 = jnp.concatenate([q_ref[f, h, pl.ds(1, 32, stride=2), :] for h in range(2)], axis=1)
    s_ref[f, 0, 8:40] = d1
    s_ref[f, 1, 8:40] = d2
    d3 = s_ref[f, 0, 9:41]
    d0 = s_ref[f, 1, 7:39]
    for k, v in enumerate((d0 - d2, d1 + d2, d2 - d1, d1 - d3)):
        u_ref[(k, *to)] = v.astype(BF)


def own_row(ok_ref, red_ref, f, r, u_ref, s_ref, q_ref):
    act = silu(red_ref[f % 2, r].astype(F32))
    if r == 8:
        act = act * ok_ref[1].astype(F32)
    prep_mid(act, f, (f, r + 1), u_ref, s_ref, q_ref)


def kernel_early(
    ok_ref, u_ref, x2_ref, f_in, w_ref, kd_ref, bf_ref, bd_ref, ks_ref, red_ref, f_ref, p_ref, u2_ref, g_ref, o_ref, s_ref, q_ref
):
    clear_shift(o_ref)
    clear_edges(s_ref)
    below = ok_ref[1].astype(F32)

    def weights(i, j):
        a, b = transformed(*(ks_ref[i, j, c].astype(F32) for c in range(3)))
        g_ref[0, i, j] = a.astype(BF)
        g_ref[1, i, j] = b.astype(BF)

    work = [lambda f=f, r=r: own_row(ok_ref, red_ref, f, r, u2_ref, s_ref, q_ref) for r in range(1, 9) for f in (2, 3)]
    work += [lambda i=i, j=j: weights(i, j) for i in range(3) for j in range(3)]
    pump = Pump(work, 6)
    first_rows(u_ref, w_ref, f_ref, o_ref, PAIR01, 15, 3, below, x2_ref.at[0:2], bf_ref[...], pump)
    out = down_conv(f_ref, kd_ref, pump)
    for q in range(2):
        p_ref[q] = (out[q] + bd_ref[...]).reshape(9, 64, 256)


def kernel_join(p_ref, z_ref, red_ref, dn_ref):
    for q in range(2):
        for r in range(9):
            red_ref[q, r] = (p_ref[q, r] + z_ref[q, r].astype(F32)).astype(BF)
        for n in range(2):
            dn_ref[q, n] = red_ref[q, 7 + n]


def taps(ks_ref, g_ref, k, i):
    if k == 0 or k == 3:
        return jnp.concatenate([ks_ref[i, j, 2 * (k // 3)] for j in range(3)], axis=0)
    return g_ref[k - 1, i].reshape(768, 256)


def columns(t_ref, at, y0, y1):
    for h in range(2):
        lanes = slice(h * 128, h * 128 + 128)
        t_ref[(*at, h, pl.ds(0, 32, stride=2), slice(None))] = y0[:, lanes]
        t_ref[(*at, h, pl.ds(1, 32, stride=2), slice(None))] = y1[:, lanes]


def frames_lhs(u_ref, k, f, count, r0, rows):
    return jnp.concatenate(
        [u_ref[k, f : f + count, r0 + j : r0 + j + rows].reshape(count * rows * 32, 256) for j in range(3)], axis=1
    )


def mixed(ms, rows):
    y0 = (ms[1] + ms[2] + ms[0]).reshape(rows, 32, 256)
    y1 = (ms[1] - ms[2] - ms[3]).reshape(rows, 32, 256)
    return y0, y1


def halo_rows(ok_ref, halo_ref, red_ref, frames, u_ref, s_ref, q_ref):
    for n, f in enumerate(frames):
        own = red_ref[n, 0].astype(F32)
        above = jnp.where(ok_ref[0] > 0, halo_ref[n, 1].astype(F32), own)
        prep_mid(silu(halo_ref[n, 0].astype(F32)), f, (f, 0), u_ref, s_ref, q_ref)
        prep_mid(silu(above), f, (f, 1), u_ref, s_ref, q_ref)


def kernel_next(ok_ref, u_in, halo_ref, red_ref, ks_ref, g_ref, u_ref, zl_ref, s_ref, q_ref, t_ref):
    clear_edges(s_ref)
    halo_rows(ok_ref, halo_ref, red_ref, (2, 3), u_ref, s_ref, q_ref)
    ms = ([], [])
    for k in range(4):
        d0 = jnp.dot(frames_lhs(u_ref, k, 2, 2, 0, 8), taps(ks_ref, g_ref, k, 0), preferred_element_type=F32)
        d1 = jnp.dot(frames_lhs(u_ref, k, 3, 1, 0, 8), taps(ks_ref, g_ref, k, 1), preferred_element_type=F32)
        ms[0].append(d0[:256] + d1)
        ms[1].append(d0[256:])
    for f in range(2):
        y0, y1 = mixed(ms[f], 8)
        for r in range(8):
            columns(t_ref, (f, r), y0[r], y1[r])
            for h in range(2):
                zl_ref[f, r, :, h * 128 : h * 128 + 128] = t_ref[f, r, h].astype(BF)


def kernel_same(ok_ref, u_in, red_ref, ks_ref, g_ref, u_ref, y_ref, s_ref, q_ref):
    clear_edges(s_ref)
    work = [lambda f=f, r=r: own_row(ok_ref, red_ref, f, r, u_ref, s_ref, q_ref) for r in range(1, 9) for f in (0, 1)]
    pump = Pump(work, 4)
    ms = ([], [])
    for k in range(4):
        d2 = jnp.dot(frames_lhs(u_ref, k, 2, 2, 0, 8), taps(ks_ref, g_ref, k, 2), preferred_element_type=F32)
        d1 = jnp.dot(frames_lhs(u_ref, k, 2, 1, 0, 8), taps(ks_ref, g_ref, k, 1), preferred_element_type=F32)
        ms[0].append(d2[:256])
        ms[1].append(d2[256:] + d1)
        pump()
    for f in range(2):
        y0, y1 = mixed(ms[f], 8)
        for r in range(8):
            columns(y_ref, (f, r), y0[r], y1[r])


def kernel_last(
    ok_ref, u_in, halo01_ref, halo23_ref, red01_ref, red23_ref, y_ref, zl_ref, ks_ref, g_ref, bs_ref,
    lat_ref, u_ref, s_ref, q_ref, t_ref, out_ref, sem,
):
    clear_edges(s_ref)
    halo_rows(ok_ref, halo01_ref, red01_ref, (0, 1), u_ref, s_ref, q_ref)
    inner = ok_ref[0] > 0
    copies = []
    for r0 in range(0, 8, STEP):
        n = STEP * 32
        ms = ([], [], [], [])
        for k in range(4):
            lhs = frames_lhs(u_ref, k, 0, 2, r0, STEP)
            e0, e1, e2 = (jnp.dot(lhs, taps(ks_ref, g_ref, k, i), preferred_element_type=F32) for i in range(3))
            ms[0].append(e2[:n])
            ms[1].append(e2[n:] + e1[:n])
            ms[2].append(e1[n:] + e0[:n])
            ms[3].append(e0[n:])
        for f in range(4):
            y0, y1 = mixed(ms[f], STEP)
            red_ref, halo_ref = ((red01_ref, halo01_ref), (red23_ref, halo23_ref))[f // 2]
            for r in range(r0, r0 + STEP):
                columns(t_ref, (f, r), y0[r - r0], y1[r - r0])
                for h in range(2):
                    lanes = slice(h * 128, h * 128 + 128)
                    v = red_ref[f % 2, r, :, lanes].astype(F32)
                    if r == 0:
                        v = jnp.where(inner, halo_ref[f % 2, 1, :, lanes].astype(F32), v)
                    if f < 2:
                        v = v + zl_ref[f, r, :, lanes].astype(F32)
                    else:
                        v = v + y_ref[f - 2, r, h]
                    out_ref[f, r, :, lanes] = (t_ref[f, r, h] + v + bs_ref[:, lanes]).astype(BF)
            rows = pl.ds(r0, STEP)
            copies.append(pltpu.make_async_copy(out_ref.at[f, rows], lat_ref.at[f, rows], sem.at[len(copies)]))
            copies[-1].start()
    for c in copies:
        c.wait()


V = pl.BlockSpec(memory_space=pltpu.VMEM)
ANY = pl.BlockSpec(memory_space=pl.ANY)
HBM = pl.BlockSpec(memory_space=pltpu.HBM)
SM = pl.BlockSpec(memory_space=pltpu.SMEM)


def sds(*shape):
    return jax.ShapeDtypeStruct(shape, BF)


def res(*shape, dtype=BF):
    return VMEM(shape, dtype)


def keep(*xs):
    return [pltpu.with_memory_space_constraint(x, pltpu.VMEM) for x in xs]


def far(*xs):
    return [pltpu.with_memory_space_constraint(x, pltpu.HBM) for x in xs]


def call(body, name, ins, outs, scratch, flops, in_specs=None, out_specs=None, aliases=None):
    return pl.pallas_call(
        body,
        out_shape=outs,
        in_specs=in_specs or [V] * len(ins),
        out_specs=out_specs or [V] * len(outs),
        scratch_shapes=scratch,
        input_output_aliases=aliases or {},
        compiler_params=pltpu.CompilerParams(vmem_limit_bytes=LIMIT),
        cost_estimate=pl.CostEstimate(flops=flops, bytes_accessed=4 << 20, transcendentals=0),
        name=name,
    )(*ins)


def on_device(features, kf, bf, kd, bd, ks, bs):
    tm, sp = lax.axis_size("tm"), lax.axis_size("space")
    down = [(i, i + 1) for i in range(sp - 1)]
    up = [(i + 1, i) for i in range(sp - 1)]
    later = [(i, i + 1) for i in range(tm - 1)]
    at = lax.axis_index("space")
    ok = jnp.stack([(at > 0).astype(jnp.int32), (at < sp - 1).astype(jnp.int32)])

    halo = lax.ppermute(features[:, 0:3], "space", up)
    wide = [VMEM((4, 2, 80, 128), F32), VMEM((4, 128, 128), F32)]
    half = [VMEM((4, 2, 48, 256), F32), VMEM((4, 2, 64, 128), F32)]
    shift = lambda n: VMEM((2, n, 72, 128), F32)
    fshape, ushape, u2shape = (2, 2, 10, 64, 384), (4, 2, 20, 64, 256), (4, 4, 10, 32, 256)
    yshape = (2, 8, 2, 64, 128)
    u, x2, w, ksv, kdv, bfv, bdv, bsv, f45, f23, f01 = call(
        kernel_own, "own", far(features, kf, ks, kd, bf.reshape(1, 128), bd.reshape(1, 256), bs.reshape(1, 256)),
        [
            res(*ushape), res(4, 18, 64, 256), res(4, 3, 2, 256, 256), res(3, 3, 3, 256, 256), res(3, 3, 128, 256),
            res(1, 128, dtype=F32), res(1, 256, dtype=F32), res(1, 256, dtype=F32), *[res(*fshape)] * 3,
        ],
        [VMEM((4, 16, 128, 128), BF), VMEM((3, 3, 3, 128, 128), BF), *wide, shift(8), pltpu.SemaphoreType.DMA((10,))],
        6_000_000_000, in_specs=[HBM] * 7,
    )
    u, x2, _, part = call(
        kernel_ahead, "ahead", (ok, *keep(u, x2, f45), halo, *keep(w, kdv)),
        [res(*ushape), res(4, 18, 64, 256), res(*fshape), sds(2, 9, 64, 256)],
        [*wide, shift(3)], 2_000_000_000, in_specs=[SM] + [V] * 6, aliases={1: 0, 2: 1, 3: 2},
    )
    zpart = lax.ppermute(part, "tm", later)
    _, red23, dn23 = call(
        kernel_late, "late", (ok, *keep(u, x2, f23, w, kdv, bfv, bdv)),
        [res(*fshape), res(2, 9, 64, 256), sds(2, 2, 64, 256)],
        [shift(3)], 2_500_000_000, in_specs=[SM] + [V] * 7, aliases={3: 0},
    )
    halo23 = lax.ppermute(dn23, "space", down)
    _, p01, u2, g = call(
        kernel_early, "early", (ok, *keep(u, x2, f01, w, kdv, bfv, bdv, ksv, red23)),
        [res(*fshape), res(2, 9, 64, 256, dtype=F32), res(*u2shape), res(2, 3, 3, 256, 256)],
        [shift(3), *half], 3_000_000_000, in_specs=[SM] + [V] * 9, aliases={3: 0},
    )
    u2, zl = call(
        kernel_next, "next", (ok, *keep(u2), halo23, *keep(red23, ksv, g)),
        [res(*u2shape), sds(2, 8, 64, 256)],
        [*half, VMEM(yshape, F32)], 2_000_000_000, in_specs=[SM] + [V] * 5, aliases={1: 0},
    )
    zlat = lax.ppermute(zl, "tm", later)
    red01, dn01 = call(
        kernel_join, "join", (*keep(p01), zpart), [res(2, 9, 64, 256), sds(2, 2, 64, 256)], [], 500_000_000
    )
    halo01 = lax.ppermute(dn01, "space", down)
    u2, y = call(
        kernel_same, "same", (ok, *keep(u2, red01, ksv, g)),
        [res(*u2shape), res(*yshape, dtype=F32)],
        half, 2_000_000_000, in_specs=[SM] + [V] * 4, aliases={1: 0},
    )
    lat, _ = call(
        kernel_last, "last", (ok, *keep(u2), halo01, halo23, *keep(red01, red23, y), zlat, *keep(ksv, g, bsv)),
        [sds(4, 8, 64, 256), res(*u2shape)],
        [*half, VMEM((4, 8, 2, 64, 128), F32), VMEM((4, 8, 64, 256), BF), pltpu.SemaphoreType.DMA((4 * 8 // STEP,))],
        4_000_000_000, in_specs=[SM] + [V] * 10, out_specs=[HBM, V], aliases={1: 1},
    )
    return lat


def solution(mesh):
    in_specs = (P("tm", "space", None, None), P(), P(), P(), P(), P(), P())
    out_specs = P("tm", "space", None, None)
    return jax.shard_map(on_device, mesh=mesh, in_specs=in_specs, out_specs=out_specs, check_vma=False)
```

```python
import jax
import jax.numpy as jnp
from jax import lax
from jax.experimental import pallas as pl
from jax.experimental.pallas import tpu as pltpu
from jax.sharding import PartitionSpec as P

BF = jnp.bfloat16
F32 = jnp.float32
VMEM = pltpu.VMEM
LIMIT = 20 * 2**20
STEP = 4


def silu(v):
    h = 0.5 * v
    return h + h * jnp.tanh(h)


def clear_edges(s_ref):
    for f in range(s_ref.shape[0]):
        for e in range(2):
            s_ref[f, e, 0:8] = jnp.zeros((8, s_ref.shape[-1]), F32)
            s_ref[f, e, s_ref.shape[2] - 8 :] = jnp.zeros((8, s_ref.shape[-1]), F32)


def prep_first(x, f, r, u_ref, x2_ref, s_ref, q_ref, residual=True):
    q_ref[f] = x.astype(F32)
    even = q_ref[f, pl.ds(0, 64, stride=2), :]
    odd = q_ref[f, pl.ds(1, 64, stride=2), :]
    d1 = silu(even)
    d2 = silu(odd)
    s_ref[f, 0, 8:72] = d1
    s_ref[f, 1, 8:72] = d2
    d3 = s_ref[f, 0, 9:73]
    d0 = s_ref[f, 1, 7:71]
    lanes = slice((f % 2) * 128, (f % 2) * 128 + 128)
    for k, v in enumerate((d0 - d2, d1 + d2, d2 - d1, d1 - d3)):
        u_ref[k, f // 2, r + 4, :, lanes] = v.astype(BF)
    if residual:
        x2_ref[f, r + 3, :, 0:128] = even.astype(BF)
        x2_ref[f, r + 3, :, 128:256] = odd.astype(BF)


def transformed(g0, g1, g2):
    half = 0.5 * (g0 + g2)
    return half + 0.5 * g1, half - 0.5 * g1


class Pump:
    def __init__(self, work, slots):
        self.work, self.slots = list(work), slots

    def __call__(self):
        count = -(-len(self.work) // max(self.slots, 1))
        self.slots -= 1
        for _ in range(count):
            self.work.pop(0)()


def idle():
    pass


def first_rows(u_ref, w_ref, f_ref, o_ref, pairs, parts, masks, residual, bias, pump=idle):
    ms = []
    for k in range(4):
        lhs = jnp.concatenate(
            [
                jnp.concatenate([u_ref[k, p, g + j : g + j + n].reshape(n * 64, 256) for g, n in parts], axis=0)
                for j in range(3)
                for p, _ in pairs
            ],
            axis=1,
        )
        rhs = jnp.concatenate([w_ref[k, j, which] for j in range(3) for _, which in pairs], axis=0)
        ms.append(jnp.dot(lhs, rhs, preferred_element_type=F32))
        pump()
    both = (ms[1] + ms[2] + ms[0], ms[1] - ms[2] - ms[3])
    rows = [g + n for g, count in parts for n in range(count)]
    for q in range(2):
        for e in range(2):
            lanes = slice(e * 128, e * 128 + 128)
            y = both[e][:, q * 128 : q * 128 + 128].reshape(len(rows), 64, 128)
            for n, g in enumerate(rows):
                row = y[n]
                if residual is not None:
                    row = row + residual[q, g, :, lanes].astype(F32) + bias
                if g < 3:
                    row = row * masks[0]
                elif g > 18:
                    row = row * masks[1]
                f_ref[q, g % 2, g // 2, :, lanes] = row.astype(BF)
                if e == 1:
                    o_ref[q, n, 8:72] = row
                    f_ref[q, g % 2, g // 2, :, 256:384] = o_ref[q, n, 7:71].astype(BF)


def clear_shift(o_ref):
    for q in range(2):
        for n in range(o_ref.shape[1]):
            o_ref[q, n, 0:8] = jnp.zeros((8, 128), F32)


def down_conv(f_ref, kd_ref, pump=idle):
    rhs = jnp.concatenate([kd_ref[j, c] for j in range(3) for c in (1, 2, 0)], axis=0)
    out = []
    for q in range(2):
        lhs = jnp.concatenate(
            [
                f_ref[q, 0, 0:10].reshape(640, 384),
                f_ref[q, 1, 0:10].reshape(640, 384),
                f_ref[q, 0, 1:11].reshape(640, 384),
            ],
            axis=1,
        )
        out.append(jnp.dot(lhs, rhs, preferred_element_type=F32))
        pump()
    return out


PAIR01 = ((0, 1),)
PAIR23 = ((0, 0), (1, 1))
PAIR45 = ((1, 0),)


EDGES = ((0, 4), (18, 3))


def edge_masks(ok_ref):
    return ok_ref[0, :, 0:128], ok_ref[1, :, 0:128]


def kernel_load(ok_ref, x_hbm, kf_hbm, x_ref, kf_ref, top_ref, bot_ref, sem):
    copies = [
        pltpu.make_async_copy(x_hbm.at[:, 12:16], top_ref, sem.at[0]),
        pltpu.make_async_copy(x_hbm.at[:, 0:3], bot_ref, sem.at[1]),
        pltpu.make_async_copy(x_hbm, x_ref, sem.at[2]),
        pltpu.make_async_copy(kf_hbm, kf_ref, sem.at[3]),
    ]
    for c in copies:
        c.start()
    for c in copies:
        c.wait()


def kernel_own(
    ok_ref, x_ref, kf_ref, ks_hbm, kd_hbm, bf_hbm, bd_hbm, bs_hbm,
    u_ref, x2_ref, w_ref, ks_ref, g_ref, kd_ref, bf_ref, bd_ref, bs_ref, f45_ref, f23_ref, f01_ref,
    s_ref, q_ref, o_ref, sem,
):
    pairs = ((bf_hbm, bf_ref), (ks_hbm, ks_ref), (kd_hbm, kd_ref), (bd_hbm, bd_ref), (bs_hbm, bs_ref))
    copies = [pltpu.make_async_copy(a, b, sem.at[n]) for n, (a, b) in enumerate(pairs)]
    for c in copies:
        c.start()
    clear_edges(s_ref)
    clear_shift(o_ref)

    def row(r, carry):
        for f in range(4):
            prep_first(x_ref[f, r], f, r, u_ref, x2_ref, s_ref, q_ref)
        return carry

    lax.fori_loop(0, 9, row, 0)

    def wrow(j, carry):
        zero = jnp.zeros((128, 128), BF)
        for i in range(3):
            g0, g1, g2 = (kf_ref[i, j, c] for c in range(3))
            a, b = transformed(g0.astype(F32), g1.astype(F32), g2.astype(F32))
            for k, g in enumerate((g0, a.astype(BF), b.astype(BF), g2)):
                if i == 0:
                    w_ref[k, j, 0, 0:128, 0:128] = g
                    w_ref[k, j, 0, 128:256, 128:256] = g
                    w_ref[k, j, 0, 0:128, 128:256] = zero
                    w_ref[k, j, 1, 128:256, 0:128] = zero
                elif i == 1:
                    w_ref[k, j, 0, 128:256, 0:128] = g
                    w_ref[k, j, 1, 0:128, 128:256] = g
                else:
                    w_ref[k, j, 1, 0:128, 0:128] = g
                    w_ref[k, j, 1, 128:256, 128:256] = g
        return carry

    lax.fori_loop(0, 3, wrow, 0)
    for c in copies:
        c.wait()

    def weights(i, j):
        a, b = transformed(*(ks_ref[i, j, c].astype(F32) for c in range(3)))
        g_ref[0, i, j] = a.astype(BF)
        g_ref[1, i, j] = b.astype(BF)

    rest = Pump(
        [
            lambda f=f, r=r: prep_first(x_ref[f, r], f, r, u_ref, x2_ref, s_ref, q_ref)
            for r in range(9, 16)
            for f in range(4)
        ],
        12,
    )
    late = Pump([lambda i=i, j=j: weights(i, j) for i in range(3) for j in range(3)], 12)
    for g, pump in ((4, rest), (11, late)):
        parts = ((g, 7),)
        first_rows(u_ref, w_ref, f45_ref, o_ref, PAIR45, parts, None, None, None, pump)
        first_rows(u_ref, w_ref, f23_ref, o_ref, PAIR23, parts, None, x2_ref.at[2:4], bf_ref[...], pump)
        first_rows(u_ref, w_ref, f01_ref, o_ref, PAIR01, parts, None, x2_ref.at[0:2], bf_ref[...], pump)


def kernel_ahead(
    ok_ref, u_in, x2_in, f_in, top_ref, bot_ref, w_ref, kd_ref, u_ref, x2_ref, f_ref, part_ref, s_ref, q_ref, o_ref
):
    clear_edges(s_ref)
    clear_shift(o_ref)

    def halo(f, r):
        x = top_ref[f, r + 4] if r < 0 else bot_ref[f, r - 16]
        prep_first(x, f, r, u_ref, x2_ref, s_ref, q_ref, -4 < r < 18)

    rows = (-4, -3, -2, -1, 16, 17, 18)
    for r in rows:
        for f in (2, 3):
            halo(f, r)
    pump = Pump([lambda f=f, r=r: halo(f, r) for r in rows for f in (0, 1)], 6)
    first_rows(u_ref, w_ref, f_ref, o_ref, PAIR45, EDGES, edge_masks(ok_ref), None, None, pump)
    out = down_conv(f_ref, kd_ref, pump)
    for q in range(2):
        part_ref[q] = out[q].reshape(10, 64, 256).astype(BF)


def kernel_late(ok_ref, u_ref, x2_ref, f_in, w_ref, kd_ref, bf_ref, bd_ref, f_ref, red_ref, o_ref):
    clear_shift(o_ref)
    first_rows(u_ref, w_ref, f_ref, o_ref, PAIR23, EDGES, edge_masks(ok_ref), x2_ref.at[2:4], bf_ref[...])
    out = down_conv(f_ref, kd_ref)
    for q in range(2):
        red_ref[q] = (out[q] + bd_ref[...]).astype(BF).reshape(10, 64, 256)


def kernel_early(ok_ref, u_ref, x2_ref, f_in, w_ref, kd_ref, bf_ref, bd_ref, z_ref, f_ref, red_ref, o_ref):
    clear_shift(o_ref)
    first_rows(u_ref, w_ref, f_ref, o_ref, PAIR01, EDGES, edge_masks(ok_ref), x2_ref.at[0:2], bf_ref[...])
    out = down_conv(f_ref, kd_ref)
    for q in range(2):
        red_ref[q] = (out[q] + bd_ref[...] + z_ref[q].reshape(640, 256).astype(F32)).astype(BF).reshape(10, 64, 256)


def prep_mid(act, f, to, u_ref, s_ref, q_ref):
    q_ref[f, 0] = act[:, 0:128]
    q_ref[f, 1] = act[:, 128:256]
    d1 = jnp.concatenate([q_ref[f, h, pl.ds(0, 32, stride=2), :] for h in range(2)], axis=1)
    d2 = jnp.concatenate([q_ref[f, h, pl.ds(1, 32, stride=2), :] for h in range(2)], axis=1)
    s_ref[f, 0, 8:40] = d1
    s_ref[f, 1, 8:40] = d2
    d3 = s_ref[f, 0, 9:41]
    d0 = s_ref[f, 1, 7:39]
    for k, v in enumerate((d0 - d2, d1 + d2, d2 - d1, d1 - d3)):
        u_ref[(k, *to)] = v.astype(BF)


def own_row(ok_ref, red_ref, f, r, u_ref, s_ref, q_ref):
    act = silu(red_ref[f % 2, r].astype(F32))
    if r == 0 or r == 9:
        act = act * ok_ref[r // 9]
    prep_mid(act, f, (f, r), u_ref, s_ref, q_ref)


def taps(ks_ref, g_ref, k, i):
    if k == 0 or k == 3:
        return jnp.concatenate([ks_ref[i, j, 2 * (k // 3)] for j in range(3)], axis=0)
    return g_ref[k - 1, i].reshape(768, 256)


def columns(t_ref, at, y0, y1):
    for h in range(2):
        lanes = slice(h * 128, h * 128 + 128)
        t_ref[(*at, h, pl.ds(0, 32, stride=2), slice(None))] = y0[:, lanes]
        t_ref[(*at, h, pl.ds(1, 32, stride=2), slice(None))] = y1[:, lanes]


def frames_lhs(u_ref, k, f, count, r0, rows):
    return jnp.concatenate(
        [u_ref[k, f : f + count, r0 + j : r0 + j + rows].reshape(count * rows * 32, 256) for j in range(3)], axis=1
    )


def mixed(ms, rows):
    y0 = (ms[1] + ms[2] + ms[0]).reshape(rows, 32, 256)
    y1 = (ms[1] - ms[2] - ms[3]).reshape(rows, 32, 256)
    return y0, y1


def kernel_next(ok_ref, red_ref, ks_ref, g_ref, u_ref, zl_ref, s_ref, q_ref, t_ref):
    clear_edges(s_ref)
    for r in range(10):
        for f in (2, 3):
            own_row(ok_ref, red_ref, f, r, u_ref, s_ref, q_ref)
    ms = ([], [])
    for k in range(4):
        d0 = jnp.dot(frames_lhs(u_ref, k, 2, 2, 0, 8), taps(ks_ref, g_ref, k, 0), preferred_element_type=F32)
        d1 = jnp.dot(frames_lhs(u_ref, k, 3, 1, 0, 8), taps(ks_ref, g_ref, k, 1), preferred_element_type=F32)
        ms[0].append(d0[:256] + d1)
        ms[1].append(d0[256:])
    for f in range(2):
        y0, y1 = mixed(ms[f], 8)
        for r in range(8):
            columns(t_ref, (f, r), y0[r], y1[r])
            for h in range(2):
                zl_ref[f, r, :, h * 128 : h * 128 + 128] = t_ref[f, r, h].astype(BF)


def kernel_same(ok_ref, u_in, red_ref, ks_ref, g_ref, u_ref, y_ref, s_ref, q_ref):
    clear_edges(s_ref)
    work = [lambda f=f, r=r: own_row(ok_ref, red_ref, f, r, u_ref, s_ref, q_ref) for r in range(10) for f in (0, 1)]
    pump = Pump(work, 4)
    ms = ([], [])
    for k in range(4):
        d2 = jnp.dot(frames_lhs(u_ref, k, 2, 2, 0, 8), taps(ks_ref, g_ref, k, 2), preferred_element_type=F32)
        d1 = jnp.dot(frames_lhs(u_ref, k, 2, 1, 0, 8), taps(ks_ref, g_ref, k, 1), preferred_element_type=F32)
        ms[0].append(d2[:256])
        ms[1].append(d2[256:] + d1)
        pump()
    for f in range(2):
        y0, y1 = mixed(ms[f], 8)
        for r in range(8):
            columns(y_ref, (f, r), y0[r], y1[r])


def kernel_last(u_ref, red01_ref, red23_ref, y_ref, zl_ref, ks_ref, g_ref, bs_ref, lat_ref, t_ref, out_ref, sem):
    copies = []
    for r0 in range(0, 8, STEP):
        n = STEP * 32
        ms = ([], [], [], [])
        for k in range(4):
            lhs = frames_lhs(u_ref, k, 0, 2, r0, STEP)
            e0, e1, e2 = (jnp.dot(lhs, taps(ks_ref, g_ref, k, i), preferred_element_type=F32) for i in range(3))
            ms[0].append(e2[:n])
            ms[1].append(e2[n:] + e1[:n])
            ms[2].append(e1[n:] + e0[:n])
            ms[3].append(e0[n:])
        for f in range(4):
            y0, y1 = mixed(ms[f], STEP)
            red_ref = (red01_ref, red23_ref)[f // 2]
            for r in range(r0, r0 + STEP):
                columns(t_ref, (f, r), y0[r - r0], y1[r - r0])
                for h in range(2):
                    lanes = slice(h * 128, h * 128 + 128)
                    v = red_ref[f % 2, r + 1, :, lanes].astype(F32)
                    if f < 2:
                        v = v + zl_ref[f, r, :, lanes].astype(F32)
                    else:
                        v = v + y_ref[f - 2, r, h]
                    out_ref[f, r, :, lanes] = (t_ref[f, r, h] + v + bs_ref[:, lanes]).astype(BF)
            rows = pl.ds(r0, STEP)
            copies.append(pltpu.make_async_copy(out_ref.at[f, rows], lat_ref.at[f, rows], sem.at[len(copies)]))
            copies[-1].start()
    for c in copies:
        c.wait()


V = pl.BlockSpec(memory_space=pltpu.VMEM)
HBM = pl.BlockSpec(memory_space=pltpu.HBM)


def sds(*shape):
    return jax.ShapeDtypeStruct(shape, BF)


def res(*shape, dtype=BF):
    return VMEM(shape, dtype)


def keep(*xs):
    return [pltpu.with_memory_space_constraint(x, pltpu.VMEM) for x in xs]


def far(*xs):
    return [pltpu.with_memory_space_constraint(x, pltpu.HBM) for x in xs]


def call(body, name, ins, outs, scratch, flops, in_specs=None, out_specs=None, aliases=None):
    return pl.pallas_call(
        body,
        out_shape=outs,
        in_specs=in_specs or [V] * len(ins),
        out_specs=out_specs or [V] * len(outs),
        scratch_shapes=scratch,
        input_output_aliases=aliases or {},
        compiler_params=pltpu.CompilerParams(vmem_limit_bytes=LIMIT),
        cost_estimate=pl.CostEstimate(flops=flops, bytes_accessed=4 << 20, transcendentals=0),
        name=name,
    )(*ins)


def on_device(features, kf, bf, kd, bd, ks, bs):
    tm, sp = lax.axis_size("tm"), lax.axis_size("space")
    down = [(i, i + 1) for i in range(sp - 1)]
    up = [(i + 1, i) for i in range(sp - 1)]
    later = [(i, i + 1) for i in range(tm - 1)]
    at = lax.axis_index("space")
    ok = jnp.stack([at > 0, at < sp - 1]).astype(F32).reshape(2, 1, 1) * jnp.ones((1, 1, 256), F32)

    wide = [VMEM((4, 2, 80, 128), F32), VMEM((4, 128, 128), F32)]
    half = [VMEM((4, 2, 48, 256), F32), VMEM((4, 2, 64, 128), F32)]
    shift = VMEM((2, 7, 72, 128), F32)
    fshape, ushape, x2shape, u2shape = (2, 2, 11, 64, 384), (4, 2, 23, 64, 256), (4, 21, 64, 256), (4, 4, 10, 32, 256)
    yshape, rshape = (2, 8, 2, 64, 128), (2, 10, 64, 256)
    xv, kfv, edge_dn, edge_up = call(
        kernel_load, "load", (*keep(ok), *far(features, kf)),
        [res(4, 16, 128, 128), res(3, 3, 3, 128, 128), sds(4, 4, 128, 128), sds(4, 3, 128, 128)],
        [pltpu.SemaphoreType.DMA((4,))], 100_000_000, in_specs=[V] + [HBM] * 2,
    )
    top = lax.ppermute(edge_dn, "space", down)
    bot = lax.ppermute(edge_up, "space", up)
    u, x2, w, ksv, g, kdv, bfv, bdv, bsv, f45, f23, f01 = call(
        kernel_own, "own", (*keep(ok, xv, kfv), *far(ks, kd, bf.reshape(1, 128), bd.reshape(1, 256), bs.reshape(1, 256))),
        [
            res(*ushape), res(*x2shape), res(4, 3, 2, 256, 256), res(3, 3, 3, 256, 256), res(2, 3, 3, 256, 256),
            res(3, 3, 128, 256), res(1, 128, dtype=F32), res(1, 256, dtype=F32), res(1, 256, dtype=F32),
            *[res(*fshape)] * 3,
        ],
        [*wide, shift, pltpu.SemaphoreType.DMA((5,))], 8_000_000_000, in_specs=[V] * 3 + [HBM] * 5,
    )
    u, x2, _, part = call(
        kernel_ahead, "ahead", (*keep(ok, u, x2, f45), top, bot, *keep(w, kdv)),
        [res(*ushape), res(*x2shape), res(*fshape), sds(*rshape)],
        [*wide, shift], 2_000_000_000, in_specs=[V] + [V] * 7, aliases={1: 0, 2: 1, 3: 2},
    )
    zpart = lax.ppermute(part, "tm", later)
    _, red23 = call(
        kernel_late, "late", keep(ok, u, x2, f23, w, kdv, bfv, bdv), [res(*fshape), res(*rshape)],
        [shift], 2_500_000_000, in_specs=[V] + [V] * 7, aliases={3: 0},
    )
    u2, zl = call(
        kernel_next, "next", keep(ok, red23, ksv, g), [res(*u2shape), sds(2, 8, 64, 256)],
        [*half, VMEM(yshape, F32)], 2_000_000_000, in_specs=[V] + [V] * 3,
    )
    zlat = lax.ppermute(zl, "tm", later)
    _, red01 = call(
        kernel_early, "early", (*keep(ok, u, x2, f01, w, kdv, bfv, bdv), zpart), [res(*fshape), res(*rshape)],
        [shift], 2_500_000_000, in_specs=[V] + [V] * 8, aliases={3: 0},
    )
    u2, y = call(
        kernel_same, "same", keep(ok, u2, red01, ksv, g), [res(*u2shape), res(*yshape, dtype=F32)],
        half, 2_000_000_000, in_specs=[V] + [V] * 4, aliases={1: 0},
    )
    (lat,) = call(
        kernel_last, "last", (*keep(u2, red01, red23, y), zlat, *keep(ksv, g, bsv)), [sds(4, 8, 64, 256)],
        [VMEM((4, 8, 2, 64, 128), F32), VMEM((4, 8, 64, 256), BF), pltpu.SemaphoreType.DMA((4 * 8 // STEP,))],
        4_000_000_000, in_specs=[V] * 8, out_specs=[HBM],
    )
    return lat


def solution(mesh):
    in_specs = (P("tm", "space", None, None), P(), P(), P(), P(), P(), P())
    out_specs = P("tm", "space", None, None)
    return jax.shard_map(on_device, mesh=mesh, in_specs=in_specs, out_specs=out_specs, check_vma=False)
```

```python
import jax
import jax.numpy as jnp
from jax import lax
from jax.experimental import pallas as pl
from jax.experimental.pallas import tpu as pltpu
from jax.sharding import PartitionSpec as P


BF = jnp.bfloat16
F32 = jnp.float32
VMEM = pltpu.VMEM
LIMIT = 12 * 2**20
STEP = 4


def silu(v):
    h = 0.5 * v
    return h + h * jnp.tanh(h)


def clear_edges(s_ref):
    for f in range(s_ref.shape[0]):
        for e in range(2):
            s_ref[f, e, 0:8] = jnp.zeros((8, s_ref.shape[-1]), F32)
            s_ref[f, e, s_ref.shape[2] - 8 :] = jnp.zeros((8, s_ref.shape[-1]), F32)


def prep_first(x, f, r, u_ref, x2_ref, s_ref, q_ref, residual=True):
    q_ref[f] = x.astype(F32)
    even = q_ref[f, pl.ds(0, 64, stride=2), :]
    odd = q_ref[f, pl.ds(1, 64, stride=2), :]
    d1 = silu(even)
    d2 = silu(odd)
    s_ref[f, 0, 8:72] = d1
    s_ref[f, 1, 8:72] = d2
    d3 = s_ref[f, 0, 9:73]
    d0 = s_ref[f, 1, 7:71]
    lanes = slice((f % 2) * 128, (f % 2) * 128 + 128)
    for k, v in enumerate((d0 - d2, d1 + d2, d2 - d1, d1 - d3)):
        u_ref[k, f // 2, r + 4, :, lanes] = v.astype(BF)
    if residual:
        x2_ref[f, r + 3, :, 0:128] = even.astype(BF)
        x2_ref[f, r + 3, :, 128:256] = odd.astype(BF)


def transformed(g0, g1, g2):
    half = 0.5 * (g0 + g2)
    return half + 0.5 * g1, half - 0.5 * g1


class Pump:
    def __init__(self, work, slots):
        self.work, self.slots = list(work), slots

    def __call__(self):
        count = -(-len(self.work) // max(self.slots, 1))
        self.slots -= 1
        for _ in range(count):
            self.work.pop(0)()


def idle():
    pass


def first_rows(u_ref, w_ref, f_ref, o_ref, pairs, parts, masks, residual, bias, pump=idle):
    ms = []
    for k in range(4):
        lhs = jnp.concatenate(
            [
                jnp.concatenate([u_ref[k, p, g + j : g + j + n].reshape(n * 64, 256) for g, n in parts], axis=0)
                for j in range(3)
                for p, _ in pairs
            ],
            axis=1,
        )
        rhs = jnp.concatenate([w_ref[k, j, which] for j in range(3) for _, which in pairs], axis=0)
        ms.append(jnp.dot(lhs, rhs, preferred_element_type=F32))
        pump()
    both = (ms[1] + ms[2] + ms[0], ms[1] - ms[2] - ms[3])
    rows = [g + n for g, count in parts for n in range(count)]
    for q in range(2):
        for e in range(2):
            lanes = slice(e * 128, e * 128 + 128)
            y = both[e][:, q * 128 : q * 128 + 128].reshape(len(rows), 64, 128)
            for n, g in enumerate(rows):
                row = y[n]
                if residual is not None:
                    row = row + residual[q, g, :, lanes].astype(F32) + bias
                if g < 3:
                    row = row * masks[0]
                elif g > 18:
                    row = row * masks[1]
                f_ref[q, g % 2, g // 2, :, lanes] = row.astype(BF)
                if e == 1:
                    o_ref[q, n, 8:72] = row
                    f_ref[q, g % 2, g // 2, :, 256:384] = o_ref[q, n, 7:71].astype(BF)


def clear_shift(o_ref):
    for q in range(2):
        for n in range(o_ref.shape[1]):
            o_ref[q, n, 0:8] = jnp.zeros((8, 128), F32)


def down_conv(f_ref, kd_ref, parts, pump=idle):
    rhs = jnp.concatenate([kd_ref[j, c] for j in range(3) for c in (1, 2, 0)], axis=0)
    rows = [m + n for m, count in parts for n in range(count)]
    out = []
    for q in range(2):
        lhs = jnp.concatenate(
            [
                jnp.concatenate([f_ref[q, e, m + d : m + d + n].reshape(n * 64, 384) for m, n in parts], axis=0)
                for e, d in ((0, 0), (1, 0), (0, 1))
            ],
            axis=1,
        )
        y = jnp.dot(lhs, rhs, preferred_element_type=F32).reshape(len(rows), 64, 256)
        out += [(q, m, y[n]) for n, m in enumerate(rows)]
        pump()
    return out


PAIR01 = ((0, 1),)
PAIR23 = ((0, 0), (1, 1))
PAIR45 = ((1, 0),)


EDGES = ((0, 4), (18, 3))
INSIDE = ((2, 6),)
OUTSIDE = ((0, 2), (8, 2))


def edge_masks(ok_ref):
    return ok_ref[0, :, 0:128], ok_ref[1, :, 0:128]


def kernel_load(ok_ref, x_hbm, kf_hbm, x_ref, kf_ref, top_ref, bot_ref, sem):
    copies = [
        pltpu.make_async_copy(x_hbm.at[:, 12:16], top_ref, sem.at[0]),
        pltpu.make_async_copy(x_hbm.at[:, 0:3], bot_ref, sem.at[1]),
        pltpu.make_async_copy(x_hbm, x_ref, sem.at[2]),
        pltpu.make_async_copy(kf_hbm, kf_ref, sem.at[3]),
    ]
    for c in copies:
        c.start()
    for c in copies:
        c.wait()


def kernel_own(
    ok_ref, x_ref, kf_ref, ks_hbm, kd_hbm, bf_hbm, bd_hbm, bs_hbm,
    u_ref, x2_ref, w_ref, ks_ref, g_ref, kd_ref, bf_ref, bd_ref, bs_ref, f45_ref, f23_ref, f01_ref,
    part_ref, red_ref, p_ref, u2_ref, s_ref, q_ref, o_ref, s2_ref, q2_ref, sem,
):
    pairs = ((bf_hbm, bf_ref), (ks_hbm, ks_ref), (kd_hbm, kd_ref), (bd_hbm, bd_ref), (bs_hbm, bs_ref))
    copies = [pltpu.make_async_copy(a, b, sem.at[n]) for n, (a, b) in enumerate(pairs)]
    for c in copies:
        c.start()
    clear_edges(s_ref)
    clear_edges(s2_ref)
    clear_shift(o_ref)

    def row(r, carry):
        for f in range(4):
            prep_first(x_ref[f, r], f, r, u_ref, x2_ref, s_ref, q_ref)
        return carry

    lax.fori_loop(0, 9, row, 0)

    def wrow(j, carry):
        zero = jnp.zeros((128, 128), BF)
        for i in range(3):
            g0, g1, g2 = (kf_ref[i, j, c] for c in range(3))
            a, b = transformed(g0.astype(F32), g1.astype(F32), g2.astype(F32))
            for k, g in enumerate((g0, a.astype(BF), b.astype(BF), g2)):
                if i == 0:
                    w_ref[k, j, 0, 0:128, 0:128] = g
                    w_ref[k, j, 0, 128:256, 128:256] = g
                    w_ref[k, j, 0, 0:128, 128:256] = zero
                    w_ref[k, j, 1, 128:256, 0:128] = zero
                elif i == 1:
                    w_ref[k, j, 0, 128:256, 0:128] = g
                    w_ref[k, j, 1, 0:128, 128:256] = g
                else:
                    w_ref[k, j, 1, 0:128, 0:128] = g
                    w_ref[k, j, 1, 128:256, 128:256] = g
        return carry

    lax.fori_loop(0, 3, wrow, 0)
    for c in copies:
        c.wait()

    def weights(i, j):
        a, b = transformed(*(ks_ref[i, j, c].astype(F32) for c in range(3)))
        g_ref[0, i, j] = a.astype(BF)
        g_ref[1, i, j] = b.astype(BF)

    rest = Pump(
        [
            lambda f=f, r=r: prep_first(x_ref[f, r], f, r, u_ref, x2_ref, s_ref, q_ref)
            for r in range(9, 16)
            for f in range(4)
        ],
        12,
    )
    gains = Pump([lambda i=i, j=j: weights(i, j) for i in range(3) for j in range(3)], 6)
    mids = Pump(
        [lambda f=f, r=r: own_row(ok_ref, red_ref, f, r, u2_ref, s2_ref, q2_ref) for r in range(2, 8) for f in (2, 3)], 8
    )
    bias, parts = bf_ref[...], ((4, 7),)
    first_rows(u_ref, w_ref, f45_ref, o_ref, PAIR45, parts, None, None, None, rest)
    first_rows(u_ref, w_ref, f23_ref, o_ref, PAIR23, parts, None, x2_ref.at[2:4], bias, rest)
    first_rows(u_ref, w_ref, f01_ref, o_ref, PAIR01, parts, None, x2_ref.at[0:2], bias, rest)
    parts = ((11, 7),)
    first_rows(u_ref, w_ref, f23_ref, o_ref, PAIR23, parts, None, x2_ref.at[2:4], bias, gains)
    for q, m, y in down_conv(f23_ref, kd_ref, INSIDE, gains):
        red_ref[q, m] = (y + bd_ref[...]).astype(BF)
    first_rows(u_ref, w_ref, f45_ref, o_ref, PAIR45, parts, None, None, None, mids)
    first_rows(u_ref, w_ref, f01_ref, o_ref, PAIR01, parts, None, x2_ref.at[0:2], bias, mids)
    for q, m, y in down_conv(f45_ref, kd_ref, INSIDE):
        part_ref[q, m] = y.astype(BF)
    for q, m, y in down_conv(f01_ref, kd_ref, INSIDE):
        p_ref[q, m] = y + bd_ref[...]


def kernel_ahead(
    ok_ref, u_in, x2_in, f_in, part_in, top_ref, bot_ref, w_ref, kd_ref, u_ref, x2_ref, f_ref, part_ref, s_ref, q_ref, o_ref
):
    clear_edges(s_ref)
    clear_shift(o_ref)

    def halo(f, r):
        x = top_ref[f, r + 4] if r < 0 else bot_ref[f, r - 16]
        prep_first(x, f, r, u_ref, x2_ref, s_ref, q_ref, -4 < r < 18)

    rows = (-4, -3, -2, -1, 16, 17, 18)
    for r in rows:
        for f in (2, 3):
            halo(f, r)
    pump = Pump([lambda f=f, r=r: halo(f, r) for r in rows for f in (0, 1)], 6)
    first_rows(u_ref, w_ref, f_ref, o_ref, PAIR45, EDGES, edge_masks(ok_ref), None, None, pump)
    for q, m, y in down_conv(f_ref, kd_ref, OUTSIDE, pump):
        part_ref[q, m] = y.astype(BF)


def kernel_late(ok_ref, u_ref, x2_ref, f_in, red_in, w_ref, kd_ref, bf_ref, bd_ref, f_ref, red_ref, o_ref):
    clear_shift(o_ref)
    first_rows(u_ref, w_ref, f_ref, o_ref, PAIR23, EDGES, edge_masks(ok_ref), x2_ref.at[2:4], bf_ref[...])
    for q, m, y in down_conv(f_ref, kd_ref, OUTSIDE):
        red_ref[q, m] = (y + bd_ref[...]).astype(BF)


def kernel_early(ok_ref, u_ref, x2_ref, f_in, p_in, w_ref, kd_ref, bf_ref, bd_ref, f_ref, p_ref, o_ref):
    clear_shift(o_ref)
    first_rows(u_ref, w_ref, f_ref, o_ref, PAIR01, EDGES, edge_masks(ok_ref), x2_ref.at[0:2], bf_ref[...])
    for q, m, y in down_conv(f_ref, kd_ref, OUTSIDE):
        p_ref[q, m] = y + bd_ref[...]


def prep_mid(act, f, to, u_ref, s_ref, q_ref):
    q_ref[f, 0] = act[:, 0:128]
    q_ref[f, 1] = act[:, 128:256]
    d1 = jnp.concatenate([q_ref[f, h, pl.ds(0, 32, stride=2), :] for h in range(2)], axis=1)
    d2 = jnp.concatenate([q_ref[f, h, pl.ds(1, 32, stride=2), :] for h in range(2)], axis=1)
    s_ref[f, 0, 8:40] = d1
    s_ref[f, 1, 8:40] = d2
    d3 = s_ref[f, 0, 9:41]
    d0 = s_ref[f, 1, 7:39]
    for k, v in enumerate((d0 - d2, d1 + d2, d2 - d1, d1 - d3)):
        u_ref[(k, *to)] = v.astype(BF)


def own_row(ok_ref, red_ref, f, r, u_ref, s_ref, q_ref):
    act = silu(red_ref[f % 2, r].astype(F32))
    if r == 0 or r == 9:
        act = act * ok_ref[r // 9]
    prep_mid(act, f, (f, r), u_ref, s_ref, q_ref)


def taps(ks_ref, g_ref, k, i):
    if k == 0 or k == 3:
        return jnp.concatenate([ks_ref[i, j, 2 * (k // 3)] for j in range(3)], axis=0)
    return g_ref[k - 1, i].reshape(768, 256)


def columns(t_ref, at, y0, y1):
    for h in range(2):
        lanes = slice(h * 128, h * 128 + 128)
        t_ref[(*at, h, pl.ds(0, 32, stride=2), slice(None))] = y0[:, lanes]
        t_ref[(*at, h, pl.ds(1, 32, stride=2), slice(None))] = y1[:, lanes]


def frames_lhs(u_ref, k, f, count, r0, rows):
    return jnp.concatenate(
        [u_ref[k, f : f + count, r0 + j : r0 + j + rows].reshape(count * rows * 32, 256) for j in range(3)], axis=1
    )


def mixed(ms, rows):
    y0 = (ms[1] + ms[2] + ms[0]).reshape(rows, 32, 256)
    y1 = (ms[1] - ms[2] - ms[3]).reshape(rows, 32, 256)
    return y0, y1


def kernel_next(ok_ref, u_in, red_ref, ks_ref, g_ref, u_ref, zl_ref, s_ref, q_ref, t_ref):
    clear_edges(s_ref)
    for r in (0, 1, 8, 9):
        for f in (2, 3):
            own_row(ok_ref, red_ref, f, r, u_ref, s_ref, q_ref)
    ms = ([], [])
    for k in range(4):
        d0 = jnp.dot(frames_lhs(u_ref, k, 2, 2, 0, 8), taps(ks_ref, g_ref, k, 0), preferred_element_type=F32)
        d1 = jnp.dot(frames_lhs(u_ref, k, 3, 1, 0, 8), taps(ks_ref, g_ref, k, 1), preferred_element_type=F32)
        ms[0].append(d0[:256] + d1)
        ms[1].append(d0[256:])
    for f in range(2):
        y0, y1 = mixed(ms[f], 8)
        for r in range(8):
            columns(t_ref, (f, r), y0[r], y1[r])
            for h in range(2):
                zl_ref[f, r, :, h * 128 : h * 128 + 128] = t_ref[f, r, h].astype(BF)


def kernel_same(ok_ref, u_in, p_ref, z_ref, ks_ref, g_ref, u_ref, red_ref, y_ref, s_ref, q_ref):
    clear_edges(s_ref)

    def joined(f, r):
        red_ref[f, r] = (p_ref[f, r] + z_ref[f, r].astype(F32)).astype(BF)
        own_row(ok_ref, red_ref, f, r, u_ref, s_ref, q_ref)

    pump = Pump([lambda f=f, r=r: joined(f, r) for r in range(10) for f in (0, 1)], 4)
    ms = ([], [])
    for k in range(4):
        d2 = jnp.dot(frames_lhs(u_ref, k, 2, 2, 0, 8), taps(ks_ref, g_ref, k, 2), preferred_element_type=F32)
        d1 = jnp.dot(frames_lhs(u_ref, k, 2, 1, 0, 8), taps(ks_ref, g_ref, k, 1), preferred_element_type=F32)
        ms[0].append(d2[:256])
        ms[1].append(d2[256:] + d1)
        pump()
    for f in range(2):
        y0, y1 = mixed(ms[f], 8)
        for r in range(8):
            columns(y_ref, (f, r), y0[r], y1[r])


def kernel_rest(u_ref, red01_ref, red23_ref, y_ref, ks_ref, g_ref, bs_ref, lat_ref, y01_ref, t_ref, out_ref, sem):
    copies = []
    for r0 in range(0, 8, STEP):
        n = STEP * 32
        ms = ([], [], [], [])
        for k in range(4):
            lhs = frames_lhs(u_ref, k, 0, 2, r0, STEP)
            e0, e1, e2 = (jnp.dot(lhs, taps(ks_ref, g_ref, k, i), preferred_element_type=F32) for i in range(3))
            ms[0].append(e2[:n])
            ms[1].append(e2[n:] + e1[:n])
            ms[2].append(e1[n:] + e0[:n])
            ms[3].append(e0[n:])
        for f in (2, 3, 0, 1):
            y0, y1 = mixed(ms[f], STEP)
            for r in range(r0, r0 + STEP):
                columns(t_ref, (f, r), y0[r - r0], y1[r - r0])
                for h in range(2):
                    lanes = slice(h * 128, h * 128 + 128)
                    v = t_ref[f, r, h] + (red01_ref, red23_ref)[f // 2][f % 2, r + 1, :, lanes].astype(F32) + bs_ref[:, lanes]
                    if f < 2:
                        y01_ref[f, r, :, lanes] = v
                    else:
                        out_ref[f - 2, r, :, lanes] = (v + y_ref[f - 2, r, h]).astype(BF)
            if f > 1:
                rows = pl.ds(r0, STEP)
                copies.append(pltpu.make_async_copy(out_ref.at[f - 2, rows], lat_ref.at[f, rows], sem.at[len(copies)]))
                copies[-1].start()
    for c in copies:
        c.wait()


def kernel_last(lat_in, y_ref, zl_ref, lat_ref, out_ref, sem):
    copies = []
    for f in range(2):
        for r in range(8):
            out_ref[f, r] = (y_ref[f, r] + zl_ref[f, r].astype(F32)).astype(BF)
        copies.append(pltpu.make_async_copy(out_ref.at[f], lat_ref.at[f], sem.at[f]))
        copies[-1].start()
    for c in copies:
        c.wait()


V = pl.BlockSpec(memory_space=pltpu.VMEM)
HBM = pl.BlockSpec(memory_space=pltpu.HBM)


def sds(*shape):
    return jax.ShapeDtypeStruct(shape, BF)


def res(*shape, dtype=BF):
    return VMEM(shape, dtype)


def keep(*xs):
    return [pltpu.with_memory_space_constraint(x, pltpu.VMEM) for x in xs]


def far(*xs):
    return [pltpu.with_memory_space_constraint(x, pltpu.HBM) for x in xs]


def call(body, ins, outs, scratch, flops, in_specs=None, out_specs=None, aliases=None):
    return pl.pallas_call(
        body,
        out_shape=outs,
        in_specs=in_specs or [V] * len(ins),
        out_specs=out_specs or [V] * len(outs),
        scratch_shapes=scratch,
        input_output_aliases=aliases or {},
        compiler_params=pltpu.CompilerParams(vmem_limit_bytes=LIMIT),
        cost_estimate=pl.CostEstimate(flops=flops, bytes_accessed=4 << 20, transcendentals=0),
    )(*ins)


def on_device(features, kf, bf, kd, bd, ks, bs):
    tm, sp = lax.axis_size("tm"), lax.axis_size("space")
    down = [(i, i + 1) for i in range(sp - 1)]
    up = [(i + 1, i) for i in range(sp - 1)]
    later = [(i, i + 1) for i in range(tm - 1)]
    at = lax.axis_index("space")
    ok = jnp.stack([at > 0, at < sp - 1]).astype(F32).reshape(2, 1, 1) * jnp.ones((1, 1, 256), F32)

    wide = [VMEM((4, 2, 80, 128), F32), VMEM((4, 128, 128), F32)]
    half = [VMEM((4, 2, 48, 256), F32), VMEM((4, 2, 64, 128), F32)]
    shift = VMEM((2, 7, 72, 128), F32)
    fshape, ushape, x2shape, u2shape = (2, 2, 11, 64, 384), (4, 2, 23, 64, 256), (4, 21, 64, 256), (4, 4, 10, 32, 256)
    yshape, rshape = (2, 8, 2, 64, 128), (2, 10, 64, 256)
    xv, kfv, edge_dn, edge_up = call(
        kernel_load, (*keep(ok), *far(features, kf)),
        [res(4, 16, 128, 128), res(3, 3, 3, 128, 128), sds(4, 4, 128, 128), sds(4, 3, 128, 128)],
        [pltpu.SemaphoreType.DMA((4,))], 100_000_000, in_specs=[V] + [HBM] * 2,
    )
    top = lax.ppermute(edge_dn, "space", down)
    bot = lax.ppermute(edge_up, "space", up)
    u, x2, w, ksv, g, kdv, bfv, bdv, bsv, f45, f23, f01, part, red23, p01, u2 = call(
        kernel_own, (*keep(ok, xv, kfv), *far(ks, kd, bf.reshape(1, 128), bd.reshape(1, 256), bs.reshape(1, 256))),
        [
            res(*ushape), res(*x2shape), res(4, 3, 2, 256, 256), res(3, 3, 3, 256, 256), res(2, 3, 3, 256, 256),
            res(3, 3, 128, 256), res(1, 128, dtype=F32), res(1, 256, dtype=F32), res(1, 256, dtype=F32),
            *[res(*fshape)] * 3, res(*rshape), res(*rshape), res(*rshape, dtype=F32), res(*u2shape),
        ],
        [*wide, shift, *half, pltpu.SemaphoreType.DMA((5,))], 8_000_000_000, in_specs=[V] * 3 + [HBM] * 5,
    )
    u, x2, _, part = call(
        kernel_ahead, (*keep(ok, u, x2, f45, part), top, bot, *keep(w, kdv)),
        [res(*ushape), res(*x2shape), res(*fshape), res(*rshape)],
        [*wide, shift], 2_000_000_000, aliases={1: 0, 2: 1, 3: 2, 4: 3},
    )
    zpart = lax.ppermute(part, "tm", later)
    _, red23 = call(
        kernel_late, keep(ok, u, x2, f23, red23, w, kdv, bfv, bdv), [res(*fshape), res(*rshape)],
        [shift], 2_500_000_000, aliases={3: 0, 4: 1},
    )
    u2, zl = call(
        kernel_next, keep(ok, u2, red23, ksv, g), [res(*u2shape), sds(2, 8, 64, 256)],
        [*half, VMEM(yshape, F32)], 2_000_000_000, aliases={1: 0},
    )
    zlat = lax.ppermute(zl, "tm", later)
    _, p01 = call(
        kernel_early, keep(ok, u, x2, f01, p01, w, kdv, bfv, bdv), [res(*fshape), res(*rshape, dtype=F32)],
        [shift], 2_500_000_000, aliases={3: 0, 4: 1},
    )
    u2, red01, y = call(
        kernel_same, (*keep(ok, u2, p01), zpart, *keep(ksv, g)),
        [res(*u2shape), res(*rshape), res(*yshape, dtype=F32)], half, 2_000_000_000, aliases={1: 0},
    )
    lat, y01 = call(
        kernel_rest, keep(u2, red01, red23, y, ksv, g, bsv),
        [sds(4, 8, 64, 256), res(2, 8, 64, 256, dtype=F32)],
        [VMEM((4, 8, 2, 64, 128), F32), VMEM((2, 8, 64, 256), BF), pltpu.SemaphoreType.DMA((2 * 8 // STEP,))],
        4_000_000_000, out_specs=[HBM, V],
    )
    (lat,) = call(
        kernel_last, (lat, *keep(y01), zlat), [sds(4, 8, 64, 256)],
        [VMEM((2, 8, 64, 256), BF), pltpu.SemaphoreType.DMA((2,))],
        100_000_000, in_specs=[HBM, V, V], out_specs=[HBM], aliases={0: 0},
    )
    return lat


def solution(mesh):
    in_specs = (P("tm", "space", None, None), P(), P(), P(), P(), P(), P())
    out_specs = P("tm", "space", None, None)
    return jax.shard_map(on_device, mesh=mesh, in_specs=in_specs, out_specs=out_specs, check_vma=False)
```

```python
import jax
import jax.numpy as jnp
from jax import lax
from jax.experimental import pallas as pl
from jax.experimental.pallas import tpu as pltpu
from jax.sharding import PartitionSpec as P


BF = jnp.bfloat16
F32 = jnp.float32
VMEM = pltpu.VMEM
LIMIT = 12 * 2**20
STEP = 4


def silu(v):
    h = 0.5 * v
    return h + h * jnp.tanh(h)


def clear_edges(s_ref):
    for f in range(s_ref.shape[0]):
        for e in range(2):
            s_ref[f, e, 0:8] = jnp.zeros((8, s_ref.shape[-1]), F32)
            s_ref[f, e, s_ref.shape[2] - 8 :] = jnp.zeros((8, s_ref.shape[-1]), F32)


def prep_first(x, f, r, u_ref, x2_ref, s_ref, q_ref, residual=True):
    q_ref[f] = x.astype(F32)
    even = q_ref[f, pl.ds(0, 64, stride=2), :]
    odd = q_ref[f, pl.ds(1, 64, stride=2), :]
    d1 = silu(even)
    d2 = silu(odd)
    s_ref[f, 0, 8:72] = d1
    s_ref[f, 1, 8:72] = d2
    d3 = s_ref[f, 0, 9:73]
    d0 = s_ref[f, 1, 7:71]
    lanes = slice((f % 2) * 128, (f % 2) * 128 + 128)
    for k, v in enumerate((d0 - d2, d1 + d2, d2 - d1, d1 - d3)):
        u_ref[k, f // 2, r + 4, :, lanes] = v.astype(BF)
    if residual:
        x2_ref[f, r + 3, :, 0:128] = even.astype(BF)
        x2_ref[f, r + 3, :, 128:256] = odd.astype(BF)


def transformed(g0, g1, g2):
    half = 0.5 * (g0 + g2)
    return half + 0.5 * g1, half - 0.5 * g1


class Pump:
    def __init__(self, work, slots):
        self.work, self.slots = list(work), slots

    def __call__(self):
        count = -(-len(self.work) // max(self.slots, 1))
        self.slots -= 1
        for _ in range(count):
            self.work.pop(0)()


def idle():
    pass


def first_rows(u_ref, w_ref, f_ref, o_ref, pairs, parts, masks, residual, bias, pump=idle):
    ms = []
    for k in range(4):
        lhs = jnp.concatenate(
            [
                jnp.concatenate([u_ref[k, p, g + j : g + j + n].reshape(n * 64, 256) for g, n in parts], axis=0)
                for j in range(3)
                for p, _ in pairs
            ],
            axis=1,
        )
        rhs = jnp.concatenate([w_ref[k, j, which] for j in range(3) for _, which in pairs], axis=0)
        ms.append(jnp.dot(lhs, rhs, preferred_element_type=F32))
        pump()
    both = (ms[1] + ms[2] + ms[0], ms[1] - ms[2] - ms[3])
    rows = [g + n for g, count in parts for n in range(count)]
    for q in range(2):
        for e in range(2):
            lanes = slice(e * 128, e * 128 + 128)
            y = both[e][:, q * 128 : q * 128 + 128].reshape(len(rows), 64, 128)
            for n, g in enumerate(rows):
                row = y[n]
                if residual is not None:
                    row = row + residual[q, g, :, lanes].astype(F32) + bias
                if g < 3:
                    row = row * masks[0]
                elif g > 18:
                    row = row * masks[1]
                f_ref[q, g % 2, g // 2, :, lanes] = row.astype(BF)
                if e == 1:
                    o_ref[q, n, 8:72] = row
                    f_ref[q, g % 2, g // 2, :, 256:384] = o_ref[q, n, 7:71].astype(BF)


def clear_shift(o_ref):
    for q in range(2):
        for n in range(o_ref.shape[1]):
            o_ref[q, n, 0:8] = jnp.zeros((8, 128), F32)


def down_conv(f_ref, kd_ref, parts, pump=idle):
    rhs = jnp.concatenate([kd_ref[j, c] for j in range(3) for c in (1, 2, 0)], axis=0)
    rows = [m + n for m, count in parts for n in range(count)]
    out = []
    for q in range(2):
        lhs = jnp.concatenate(
            [
                jnp.concatenate([f_ref[q, e, m + d : m + d + n].reshape(n * 64, 384) for m, n in parts], axis=0)
                for e, d in ((0, 0), (1, 0), (0, 1))
            ],
            axis=1,
        )
        y = jnp.dot(lhs, rhs, preferred_element_type=F32).reshape(len(rows), 64, 256)
        out += [(q, m, y[n]) for n, m in enumerate(rows)]
        pump()
    return out


PAIR01 = ((0, 1),)
PAIR23 = ((0, 0), (1, 1))
PAIR45 = ((1, 0),)


EDGES = ((0, 4), (18, 3))
INSIDE = ((2, 6),)
OUTSIDE = ((0, 2), (8, 2))


def edge_masks(ok_ref):
    return ok_ref[0, :, 0:128], ok_ref[1, :, 0:128]


def kernel_load(ok_ref, x_hbm, kf_hbm, x_ref, kf_ref, top_ref, bot_ref, sem):
    copies = [
        pltpu.make_async_copy(x_hbm.at[:, 12:16], top_ref, sem.at[0]),
        pltpu.make_async_copy(x_hbm.at[:, 0:3], bot_ref, sem.at[1]),
        pltpu.make_async_copy(x_hbm, x_ref, sem.at[2]),
        pltpu.make_async_copy(kf_hbm, kf_ref, sem.at[3]),
    ]
    for c in copies:
        c.start()
    for c in copies:
        c.wait()


def kernel_own(
    ok_ref, x_ref, kf_ref, ks_hbm, kd_hbm, bf_hbm, bd_hbm, bs_hbm,
    u_ref, x2_ref, w_ref, ks_ref, g_ref, kd_ref, bf_ref, bd_ref, bs_ref, f45_ref, f23_ref,
    part_ref, red_ref, u2_ref, s_ref, q_ref, o_ref, s2_ref, q2_ref, sem,
):
    pairs = ((bf_hbm, bf_ref), (ks_hbm, ks_ref), (kd_hbm, kd_ref), (bd_hbm, bd_ref), (bs_hbm, bs_ref))
    copies = [pltpu.make_async_copy(a, b, sem.at[n]) for n, (a, b) in enumerate(pairs)]
    for c in copies:
        c.start()
    clear_edges(s_ref)
    clear_edges(s2_ref)
    clear_shift(o_ref)

    def row(r, carry):
        for f in range(4):
            prep_first(x_ref[f, r], f, r, u_ref, x2_ref, s_ref, q_ref)
        return carry

    lax.fori_loop(0, 9, row, 0)

    def wrow(j, carry):
        zero = jnp.zeros((128, 128), BF)
        for i in range(3):
            g0, g1, g2 = (kf_ref[i, j, c] for c in range(3))
            a, b = transformed(g0.astype(F32), g1.astype(F32), g2.astype(F32))
            for k, g in enumerate((g0, a.astype(BF), b.astype(BF), g2)):
                if i == 0:
                    w_ref[k, j, 0, 0:128, 0:128] = g
                    w_ref[k, j, 0, 128:256, 128:256] = g
                    w_ref[k, j, 0, 0:128, 128:256] = zero
                    w_ref[k, j, 1, 128:256, 0:128] = zero
                elif i == 1:
                    w_ref[k, j, 0, 128:256, 0:128] = g
                    w_ref[k, j, 1, 0:128, 128:256] = g
                else:
                    w_ref[k, j, 1, 0:128, 0:128] = g
                    w_ref[k, j, 1, 128:256, 128:256] = g
        return carry

    lax.fori_loop(0, 3, wrow, 0)
    for c in copies:
        c.wait()

    def weights(i, j):
        a, b = transformed(*(ks_ref[i, j, c].astype(F32) for c in range(3)))
        g_ref[0, i, j] = a.astype(BF)
        g_ref[1, i, j] = b.astype(BF)

    rest = Pump(
        [
            lambda f=f, r=r: prep_first(x_ref[f, r], f, r, u_ref, x2_ref, s_ref, q_ref)
            for r in range(9, 16)
            for f in range(4)
        ],
        8,
    )
    gains = Pump([lambda i=i, j=j: weights(i, j) for i in range(3) for j in range(3)], 6)
    mids = Pump(
        [lambda f=f, r=r: own_row(ok_ref, red_ref, f, r, u2_ref, s2_ref, q2_ref) for r in range(2, 8) for f in (2, 3)], 6
    )
    bias, parts = bf_ref[...], ((4, 7),)
    first_rows(u_ref, w_ref, f45_ref, o_ref, PAIR45, parts, None, None, None, rest)
    first_rows(u_ref, w_ref, f23_ref, o_ref, PAIR23, parts, None, x2_ref.at[2:4], bias, rest)
    parts = ((11, 7),)
    first_rows(u_ref, w_ref, f23_ref, o_ref, PAIR23, parts, None, x2_ref.at[2:4], bias, gains)
    for q, m, y in down_conv(f23_ref, kd_ref, INSIDE, gains):
        red_ref[q, m] = (y + bd_ref[...]).astype(BF)
    first_rows(u_ref, w_ref, f45_ref, o_ref, PAIR45, parts, None, None, None, mids)
    for q, m, y in down_conv(f45_ref, kd_ref, INSIDE, mids):
        part_ref[q, m] = y.astype(BF)


def kernel_ahead(
    ok_ref, u_in, x2_in, f_in, part_in, top_ref, bot_ref, w_ref, kd_ref, u_ref, x2_ref, f_ref, part_ref, s_ref, q_ref, o_ref
):
    clear_edges(s_ref)
    clear_shift(o_ref)

    def halo(f, r):
        x = top_ref[f, r + 4] if r < 0 else bot_ref[f, r - 16]
        prep_first(x, f, r, u_ref, x2_ref, s_ref, q_ref, -4 < r < 18)

    rows = (-4, -3, -2, -1, 16, 17, 18)
    for r in rows:
        for f in (2, 3):
            halo(f, r)
    pump = Pump([lambda f=f, r=r: halo(f, r) for r in rows for f in (0, 1)], 6)
    first_rows(u_ref, w_ref, f_ref, o_ref, PAIR45, EDGES, edge_masks(ok_ref), None, None, pump)
    for q, m, y in down_conv(f_ref, kd_ref, OUTSIDE, pump):
        part_ref[q, m] = y.astype(BF)


def kernel_late(ok_ref, u_ref, x2_ref, f_in, red_in, w_ref, kd_ref, bf_ref, bd_ref, f_ref, red_ref, o_ref):
    clear_shift(o_ref)
    first_rows(u_ref, w_ref, f_ref, o_ref, PAIR23, EDGES, edge_masks(ok_ref), x2_ref.at[2:4], bf_ref[...])
    for q, m, y in down_conv(f_ref, kd_ref, OUTSIDE):
        red_ref[q, m] = (y + bd_ref[...]).astype(BF)


def kernel_early(ok_ref, u_ref, x2_ref, w_ref, kd_ref, bf_ref, bd_ref, p_ref, f_ref, o_ref):
    clear_shift(o_ref)
    for parts in (((0, 7),), ((7, 7),), ((14, 7),)):
        first_rows(u_ref, w_ref, f_ref, o_ref, PAIR01, parts, edge_masks(ok_ref), x2_ref.at[0:2], bf_ref[...])
    for q, m, y in down_conv(f_ref, kd_ref, ((0, 10),)):
        p_ref[q, m] = y + bd_ref[...]


def prep_mid(act, f, to, u_ref, s_ref, q_ref):
    q_ref[f, 0] = act[:, 0:128]
    q_ref[f, 1] = act[:, 128:256]
    d1 = jnp.concatenate([q_ref[f, h, pl.ds(0, 32, stride=2), :] for h in range(2)], axis=1)
    d2 = jnp.concatenate([q_ref[f, h, pl.ds(1, 32, stride=2), :] for h in range(2)], axis=1)
    s_ref[f, 0, 8:40] = d1
    s_ref[f, 1, 8:40] = d2
    d3 = s_ref[f, 0, 9:41]
    d0 = s_ref[f, 1, 7:39]
    for k, v in enumerate((d0 - d2, d1 + d2, d2 - d1, d1 - d3)):
        u_ref[(k, *to)] = v.astype(BF)


def own_row(ok_ref, red_ref, f, r, u_ref, s_ref, q_ref):
    act = silu(red_ref[f % 2, r].astype(F32))
    if r == 0 or r == 9:
        act = act * ok_ref[r // 9]
    prep_mid(act, f, (f, r), u_ref, s_ref, q_ref)


def taps(ks_ref, g_ref, k, i):
    if k == 0 or k == 3:
        return jnp.concatenate([ks_ref[i, j, 2 * (k // 3)] for j in range(3)], axis=0)
    return g_ref[k - 1, i].reshape(768, 256)


def columns(t_ref, at, y0, y1):
    for h in range(2):
        lanes = slice(h * 128, h * 128 + 128)
        t_ref[(*at, h, pl.ds(0, 32, stride=2), slice(None))] = y0[:, lanes]
        t_ref[(*at, h, pl.ds(1, 32, stride=2), slice(None))] = y1[:, lanes]


def frames_lhs(u_ref, k, f, count, r0, rows):
    return jnp.concatenate(
        [u_ref[k, f : f + count, r0 + j : r0 + j + rows].reshape(count * rows * 32, 256) for j in range(3)], axis=1
    )


def mixed(ms, rows):
    y0 = (ms[1] + ms[2] + ms[0]).reshape(rows, 32, 256)
    y1 = (ms[1] - ms[2] - ms[3]).reshape(rows, 32, 256)
    return y0, y1


def kernel_next(ok_ref, u_in, red_ref, ks_ref, g_ref, u_ref, zl_ref, s_ref, q_ref, t_ref):
    clear_edges(s_ref)
    for r in (0, 1, 8, 9):
        for f in (2, 3):
            own_row(ok_ref, red_ref, f, r, u_ref, s_ref, q_ref)
    ms = ([], [])
    for k in range(4):
        d0 = jnp.dot(frames_lhs(u_ref, k, 2, 2, 0, 8), taps(ks_ref, g_ref, k, 0), preferred_element_type=F32)
        d1 = jnp.dot(frames_lhs(u_ref, k, 3, 1, 0, 8), taps(ks_ref, g_ref, k, 1), preferred_element_type=F32)
        ms[0].append(d0[:256] + d1)
        ms[1].append(d0[256:])
    for f in range(2):
        y0, y1 = mixed(ms[f], 8)
        for r in range(8):
            columns(t_ref, (f, r), y0[r], y1[r])
            for h in range(2):
                zl_ref[f, r, :, h * 128 : h * 128 + 128] = t_ref[f, r, h].astype(BF)


def kernel_same(ok_ref, u_in, p_ref, z_ref, ks_ref, g_ref, u_ref, red_ref, y_ref, s_ref, q_ref):
    clear_edges(s_ref)

    def joined(f, r):
        red_ref[f, r] = (p_ref[f, r] + z_ref[f, r].astype(F32)).astype(BF)
        own_row(ok_ref, red_ref, f, r, u_ref, s_ref, q_ref)

    pump = Pump([lambda f=f, r=r: joined(f, r) for r in range(10) for f in (0, 1)], 4)
    ms = ([], [])
    for k in range(4):
        d2 = jnp.dot(frames_lhs(u_ref, k, 2, 2, 0, 8), taps(ks_ref, g_ref, k, 2), preferred_element_type=F32)
        d1 = jnp.dot(frames_lhs(u_ref, k, 2, 1, 0, 8), taps(ks_ref, g_ref, k, 1), preferred_element_type=F32)
        ms[0].append(d2[:256])
        ms[1].append(d2[256:] + d1)
        pump()
    for f in range(2):
        y0, y1 = mixed(ms[f], 8)
        for r in range(8):
            columns(y_ref, (f, r), y0[r], y1[r])


def kernel_rest(u_ref, red01_ref, red23_ref, y_ref, ks_ref, g_ref, bs_ref, lat_ref, y01_ref, t_ref, out_ref, sem):
    copies = []
    for r0 in range(0, 8, STEP):
        n = STEP * 32
        ms = ([], [], [], [])
        for k in range(4):
            lhs = frames_lhs(u_ref, k, 0, 2, r0, STEP)
            e0, e1, e2 = (jnp.dot(lhs, taps(ks_ref, g_ref, k, i), preferred_element_type=F32) for i in range(3))
            ms[0].append(e2[:n])
            ms[1].append(e2[n:] + e1[:n])
            ms[2].append(e1[n:] + e0[:n])
            ms[3].append(e0[n:])
        for f in (2, 3, 0, 1):
            y0, y1 = mixed(ms[f], STEP)
            for r in range(r0, r0 + STEP):
                columns(t_ref, (f, r), y0[r - r0], y1[r - r0])
                for h in range(2):
                    lanes = slice(h * 128, h * 128 + 128)
                    v = t_ref[f, r, h] + (red01_ref, red23_ref)[f // 2][f % 2, r + 1, :, lanes].astype(F32) + bs_ref[:, lanes]
                    if f < 2:
                        y01_ref[f, r, :, lanes] = v
                    else:
                        out_ref[f - 2, r, :, lanes] = (v + y_ref[f - 2, r, h]).astype(BF)
            if f > 1:
                rows = pl.ds(r0, STEP)
                copies.append(pltpu.make_async_copy(out_ref.at[f - 2, rows], lat_ref.at[f, rows], sem.at[len(copies)]))
                copies[-1].start()
    for c in copies:
        c.wait()


def kernel_last(lat_in, y_ref, zl_ref, lat_ref, out_ref, sem):
    copies = []
    for f in range(2):
        for r in range(8):
            out_ref[f, r] = (y_ref[f, r] + zl_ref[f, r].astype(F32)).astype(BF)
        copies.append(pltpu.make_async_copy(out_ref.at[f], lat_ref.at[f], sem.at[f]))
        copies[-1].start()
    for c in copies:
        c.wait()


V = pl.BlockSpec(memory_space=pltpu.VMEM)
HBM = pl.BlockSpec(memory_space=pltpu.HBM)


def sds(*shape):
    return jax.ShapeDtypeStruct(shape, BF)


def res(*shape, dtype=BF):
    return VMEM(shape, dtype)


def keep(*xs):
    return [pltpu.with_memory_space_constraint(x, pltpu.VMEM) for x in xs]


def far(*xs):
    return [pltpu.with_memory_space_constraint(x, pltpu.HBM) for x in xs]


def call(body, ins, outs, scratch, flops, in_specs=None, out_specs=None, aliases=None):
    return pl.pallas_call(
        body,
        out_shape=outs,
        in_specs=in_specs or [V] * len(ins),
        out_specs=out_specs or [V] * len(outs),
        scratch_shapes=scratch,
        input_output_aliases=aliases or {},
        compiler_params=pltpu.CompilerParams(vmem_limit_bytes=LIMIT),
        cost_estimate=pl.CostEstimate(flops=flops, bytes_accessed=4 << 20, transcendentals=0),
    )(*ins)


def on_device(features, kf, bf, kd, bd, ks, bs):
    tm, sp = lax.axis_size("tm"), lax.axis_size("space")
    down = [(i, i + 1) for i in range(sp - 1)]
    up = [(i + 1, i) for i in range(sp - 1)]
    later = [(i, i + 1) for i in range(tm - 1)]
    at = lax.axis_index("space")
    ok = jnp.stack([at > 0, at < sp - 1]).astype(F32).reshape(2, 1, 1) * jnp.ones((1, 1, 256), F32)

    wide = [VMEM((4, 2, 80, 128), F32), VMEM((4, 128, 128), F32)]
    half = [VMEM((4, 2, 48, 256), F32), VMEM((4, 2, 64, 128), F32)]
    shift = VMEM((2, 7, 72, 128), F32)
    fshape, ushape, x2shape, u2shape = (2, 2, 11, 64, 384), (4, 2, 23, 64, 256), (4, 21, 64, 256), (4, 4, 10, 32, 256)
    yshape, rshape = (2, 8, 2, 64, 128), (2, 10, 64, 256)
    xv, kfv, edge_dn, edge_up = call(
        kernel_load, (*keep(ok), *far(features, kf)),
        [res(4, 16, 128, 128), res(3, 3, 3, 128, 128), sds(4, 4, 128, 128), sds(4, 3, 128, 128)],
        [pltpu.SemaphoreType.DMA((4,))], 100_000_000, in_specs=[V] + [HBM] * 2,
    )
    top = lax.ppermute(edge_dn, "space", down)
    bot = lax.ppermute(edge_up, "space", up)
    u, x2, w, ksv, g, kdv, bfv, bdv, bsv, f45, f23, part, red23, u2 = call(
        kernel_own, (*keep(ok, xv, kfv), *far(ks, kd, bf.reshape(1, 128), bd.reshape(1, 256), bs.reshape(1, 256))),
        [
            res(*ushape), res(*x2shape), res(4, 3, 2, 256, 256), res(3, 3, 3, 256, 256), res(2, 3, 3, 256, 256),
            res(3, 3, 128, 256), res(1, 128, dtype=F32), res(1, 256, dtype=F32), res(1, 256, dtype=F32),
            *[res(*fshape)] * 2, res(*rshape), res(*rshape), res(*u2shape),
        ],
        [*wide, shift, *half, pltpu.SemaphoreType.DMA((5,))], 8_000_000_000, in_specs=[V] * 3 + [HBM] * 5,
    )
    u, x2, _, part = call(
        kernel_ahead, (*keep(ok, u, x2, f45, part), top, bot, *keep(w, kdv)),
        [res(*ushape), res(*x2shape), res(*fshape), res(*rshape)],
        [*wide, shift], 2_000_000_000, aliases={1: 0, 2: 1, 3: 2, 4: 3},
    )
    zpart = lax.ppermute(part, "tm", later)
    _, red23 = call(
        kernel_late, keep(ok, u, x2, f23, red23, w, kdv, bfv, bdv), [res(*fshape), res(*rshape)],
        [shift], 2_500_000_000, aliases={3: 0, 4: 1},
    )
    u2, zl = call(
        kernel_next, keep(ok, u2, red23, ksv, g), [res(*u2shape), sds(2, 8, 64, 256)],
        [*half, VMEM(yshape, F32)], 2_000_000_000, aliases={1: 0},
    )
    zlat = lax.ppermute(zl, "tm", later)
    (p01,) = call(
        kernel_early, keep(ok, u, x2, w, kdv, bfv, bdv), [res(*rshape, dtype=F32)],
        [VMEM(fshape, BF), shift], 4_000_000_000,
    )
    u2, red01, y = call(
        kernel_same, (*keep(ok, u2, p01), zpart, *keep(ksv, g)),
        [res(*u2shape), res(*rshape), res(*yshape, dtype=F32)], half, 2_000_000_000, aliases={1: 0},
    )
    lat, y01 = call(
        kernel_rest, keep(u2, red01, red23, y, ksv, g, bsv),
        [sds(4, 8, 64, 256), res(2, 8, 64, 256, dtype=F32)],
        [VMEM((4, 8, 2, 64, 128), F32), VMEM((2, 8, 64, 256), BF), pltpu.SemaphoreType.DMA((2 * 8 // STEP,))],
        4_000_000_000, out_specs=[HBM, V],
    )
    (lat,) = call(
        kernel_last, (lat, *keep(y01), zlat), [sds(4, 8, 64, 256)],
        [VMEM((2, 8, 64, 256), BF), pltpu.SemaphoreType.DMA((2,))],
        100_000_000, in_specs=[HBM, V, V], out_specs=[HBM], aliases={0: 0},
    )
    return lat


def solution(mesh):
    in_specs = (P("tm", "space", None, None), P(), P(), P(), P(), P(), P())
    out_specs = P("tm", "space", None, None)
    return jax.shard_map(on_device, mesh=mesh, in_specs=in_specs, out_specs=out_specs, check_vma=False)
```

```python
import jax
import jax.numpy as jnp
from jax import lax
from jax.experimental import pallas as pl
from jax.experimental.pallas import tpu as pltpu
from jax.sharding import PartitionSpec as P


BF = jnp.bfloat16
F32 = jnp.float32
VMEM = pltpu.VMEM
LIMIT = 12 * 2**20
STEP = 8


def silu(v):
    h = 0.5 * v
    return h + h * jnp.tanh(h)


def clear_edges(s_ref):
    for f in range(s_ref.shape[0]):
        for e in range(2):
            s_ref[f, e, 0:8] = jnp.zeros((8, s_ref.shape[-1]), F32)
            s_ref[f, e, s_ref.shape[2] - 8 :] = jnp.zeros((8, s_ref.shape[-1]), F32)


def prep_first(x, f, r, u_ref, x2_ref, s_ref, q_ref, residual=True):
    q_ref[f] = x.astype(F32)
    even = q_ref[f, pl.ds(0, 64, stride=2), :]
    odd = q_ref[f, pl.ds(1, 64, stride=2), :]
    d1 = silu(even)
    d2 = silu(odd)
    s_ref[f, 0, 8:72] = d1
    s_ref[f, 1, 8:72] = d2
    d3 = s_ref[f, 0, 9:73]
    d0 = s_ref[f, 1, 7:71]
    lanes = slice((f % 2) * 128, (f % 2) * 128 + 128)
    for k, v in enumerate((d0 - d2, d1 + d2, d2 - d1, d1 - d3)):
        u_ref[k, f // 2, r + 4, :, lanes] = v.astype(BF)
    if residual:
        x2_ref[f, r + 3, :, 0:128] = even.astype(BF)
        x2_ref[f, r + 3, :, 128:256] = odd.astype(BF)


def transformed(g0, g1, g2):
    half = 0.5 * (g0 + g2)
    return half + 0.5 * g1, half - 0.5 * g1


class Pump:
    def __init__(self, work, slots):
        self.work, self.slots = list(work), slots

    def __call__(self):
        count = -(-len(self.work) // max(self.slots, 1))
        self.slots -= 1
        for _ in range(count):
            self.work.pop(0)()


def idle():
    pass


def first_rows(u_ref, w_ref, f_ref, o_ref, pairs, parts, masks, residual, bias, pump=idle):
    ms = []
    for k in range(4):
        lhs = jnp.concatenate(
            [
                jnp.concatenate([u_ref[k, p, g + j : g + j + n].reshape(n * 64, 256) for g, n in parts], axis=0)
                for j in range(3)
                for p, _ in pairs
            ],
            axis=1,
        )
        rhs = jnp.concatenate([w_ref[k, j, which] for j in range(3) for _, which in pairs], axis=0)
        ms.append(jnp.dot(lhs, rhs, preferred_element_type=F32))
        pump()
    both = (ms[1] + ms[2] + ms[0], ms[1] - ms[2] - ms[3])
    rows = [g + n for g, count in parts for n in range(count)]
    for q in range(2):
        for e in range(2):
            lanes = slice(e * 128, e * 128 + 128)
            y = both[e][:, q * 128 : q * 128 + 128].reshape(len(rows), 64, 128)
            for n, g in enumerate(rows):
                row = y[n]
                if residual is not None:
                    row = row + residual[q, g, :, lanes].astype(F32) + bias
                if g < 3:
                    row = row * masks[0]
                elif g > 18:
                    row = row * masks[1]
                f_ref[q, g % 2, g // 2, :, lanes] = row.astype(BF)
                if e == 1:
                    o_ref[q, n, 8:72] = row
                    f_ref[q, g % 2, g // 2, :, 256:384] = o_ref[q, n, 7:71].astype(BF)


def clear_shift(o_ref):
    for q in range(2):
        for n in range(o_ref.shape[1]):
            o_ref[q, n, 0:8] = jnp.zeros((8, 128), F32)


def down_conv(f_ref, kd_ref, parts, pump=idle):
    rhs = jnp.concatenate([kd_ref[j, c] for j in range(3) for c in (1, 2, 0)], axis=0)
    rows = [m + n for m, count in parts for n in range(count)]
    out = []
    for q in range(2):
        lhs = jnp.concatenate(
            [
                jnp.concatenate([f_ref[q, e, m + d : m + d + n].reshape(n * 64, 384) for m, n in parts], axis=0)
                for e, d in ((0, 0), (1, 0), (0, 1))
            ],
            axis=1,
        )
        y = jnp.dot(lhs, rhs, preferred_element_type=F32).reshape(len(rows), 64, 256)
        out += [(q, m, y[n]) for n, m in enumerate(rows)]
        pump()
    return out


PAIR01 = ((0, 1),)
PAIR23 = ((0, 0), (1, 1))
PAIR45 = ((1, 0),)


EDGES = ((0, 4), (18, 3))
INSIDE = ((2, 6),)
OUTSIDE = ((0, 2), (8, 2))


def edge_masks(ok_ref):
    return ok_ref[0, :, 0:128], ok_ref[1, :, 0:128]


def kernel_load(ok_ref, x_hbm, kf_hbm, kf_ref, top_ref, bot_ref, sem):
    copies = [
        pltpu.make_async_copy(x_hbm.at[:, 12:16], top_ref, sem.at[0]),
        pltpu.make_async_copy(x_hbm.at[:, 0:3], bot_ref, sem.at[1]),
        pltpu.make_async_copy(kf_hbm, kf_ref, sem.at[2]),
    ]
    for c in copies:
        c.start()
    for c in copies:
        c.wait()


def kernel_own(
    ok_ref, kf_ref, x_hbm, ks_hbm, kd_hbm, bf_hbm, bd_hbm, bs_hbm,
    u_ref, x2_ref, w_ref, ks_ref, g_ref, kd_ref, bf_ref, bd_ref, bs_ref, f45_ref, f23_ref,
    part_ref, red_ref, u2_ref, x_ref, s_ref, q_ref, o_ref, s2_ref, q2_ref, sem,
):
    pairs = ((bf_hbm, bf_ref), (ks_hbm, ks_ref), (kd_hbm, kd_ref), (bd_hbm, bd_ref), (bs_hbm, bs_ref))
    copies = [pltpu.make_async_copy(a, b, sem.at[n]) for n, (a, b) in enumerate(pairs)]
    xs = [
        pltpu.make_async_copy(x_hbm.at[:, 4 * n : 4 * n + 4], x_ref.at[:, 4 * n : 4 * n + 4], sem.at[5 + n])
        for n in range(4)
    ]
    for c in xs + copies:
        c.start()
    clear_edges(s_ref)
    clear_edges(s2_ref)
    clear_shift(o_ref)

    def row(r, carry):
        for f in range(4):
            prep_first(x_ref[f, r], f, r, u_ref, x2_ref, s_ref, q_ref)
        return carry

    def wrow(j, carry):
        zero = jnp.zeros((128, 128), BF)
        for i in range(3):
            g0, g1, g2 = (kf_ref[i, j, c] for c in range(3))
            a, b = transformed(g0.astype(F32), g1.astype(F32), g2.astype(F32))
            for k, g in enumerate((g0, a.astype(BF), b.astype(BF), g2)):
                if i == 0:
                    w_ref[k, j, 0, 0:128, 0:128] = g
                    w_ref[k, j, 0, 128:256, 128:256] = g
                    w_ref[k, j, 0, 0:128, 128:256] = zero
                    w_ref[k, j, 1, 128:256, 0:128] = zero
                elif i == 1:
                    w_ref[k, j, 0, 128:256, 0:128] = g
                    w_ref[k, j, 1, 0:128, 128:256] = g
                else:
                    w_ref[k, j, 1, 0:128, 0:128] = g
                    w_ref[k, j, 1, 128:256, 128:256] = g
        return carry

    lax.fori_loop(0, 3, wrow, 0)
    xs[0].wait()
    lax.fori_loop(0, 4, row, 0)
    for c in xs[1:]:
        c.wait()
    lax.fori_loop(4, 9, row, 0)
    for c in copies:
        c.wait()

    def weights(i, j):
        a, b = transformed(*(ks_ref[i, j, c].astype(F32) for c in range(3)))
        g_ref[0, i, j] = a.astype(BF)
        g_ref[1, i, j] = b.astype(BF)

    rest = Pump(
        [
            lambda f=f, r=r: prep_first(x_ref[f, r], f, r, u_ref, x2_ref, s_ref, q_ref)
            for r in range(9, 16)
            for f in range(4)
        ],
        8,
    )
    gains = Pump([lambda i=i, j=j: weights(i, j) for i in range(3) for j in range(3)], 6)
    mids = Pump(
        [lambda f=f, r=r: own_row(ok_ref, red_ref, f, r, u2_ref, s2_ref, q2_ref) for r in range(2, 8) for f in (2, 3)], 6
    )
    bias, parts = bf_ref[...], ((4, 7),)
    first_rows(u_ref, w_ref, f45_ref, o_ref, PAIR45, parts, None, None, None, rest)
    first_rows(u_ref, w_ref, f23_ref, o_ref, PAIR23, parts, None, x2_ref.at[2:4], bias, rest)
    parts = ((11, 7),)
    first_rows(u_ref, w_ref, f23_ref, o_ref, PAIR23, parts, None, x2_ref.at[2:4], bias, gains)
    for q, m, y in down_conv(f23_ref, kd_ref, INSIDE, gains):
        red_ref[q, m] = (y + bd_ref[...]).astype(BF)
    first_rows(u_ref, w_ref, f45_ref, o_ref, PAIR45, parts, None, None, None, mids)
    for q, m, y in down_conv(f45_ref, kd_ref, INSIDE, mids):
        part_ref[q, m] = y.astype(BF)


def kernel_ahead(
    ok_ref, u_in, x2_in, f_in, part_in, top_ref, bot_ref, w_ref, kd_ref, u_ref, x2_ref, f_ref, part_ref, s_ref, q_ref, o_ref
):
    clear_edges(s_ref)
    clear_shift(o_ref)

    def halo(f, r):
        x = top_ref[f, r + 4] if r < 0 else bot_ref[f, r - 16]
        prep_first(x, f, r, u_ref, x2_ref, s_ref, q_ref, -4 < r < 18)

    rows = (-4, -3, -2, -1, 16, 17, 18)
    for r in rows:
        for f in (2, 3):
            halo(f, r)
    pump = Pump([lambda f=f, r=r: halo(f, r) for r in rows for f in (0, 1)], 6)
    first_rows(u_ref, w_ref, f_ref, o_ref, PAIR45, EDGES, edge_masks(ok_ref), None, None, pump)
    for q, m, y in down_conv(f_ref, kd_ref, OUTSIDE, pump):
        part_ref[q, m] = y.astype(BF)


def kernel_late(ok_ref, u_ref, x2_ref, f_in, red_in, w_ref, kd_ref, bf_ref, bd_ref, f_ref, red_ref, o_ref):
    clear_shift(o_ref)
    first_rows(u_ref, w_ref, f_ref, o_ref, PAIR23, EDGES, edge_masks(ok_ref), x2_ref.at[2:4], bf_ref[...])
    for q, m, y in down_conv(f_ref, kd_ref, OUTSIDE):
        red_ref[q, m] = (y + bd_ref[...]).astype(BF)


def kernel_early(ok_ref, u_ref, x2_ref, w_ref, kd_ref, bf_ref, bd_ref, p_ref, f_ref, o_ref):
    clear_shift(o_ref)
    for parts in (((0, 7),), ((7, 7),), ((14, 7),)):
        first_rows(u_ref, w_ref, f_ref, o_ref, PAIR01, parts, edge_masks(ok_ref), x2_ref.at[0:2], bf_ref[...])
    for q, m, y in down_conv(f_ref, kd_ref, ((0, 10),)):
        p_ref[q, m] = y + bd_ref[...]


def prep_mid(act, f, to, u_ref, s_ref, q_ref):
    q_ref[f, 0] = act[:, 0:128]
    q_ref[f, 1] = act[:, 128:256]
    d1 = jnp.concatenate([q_ref[f, h, pl.ds(0, 32, stride=2), :] for h in range(2)], axis=1)
    d2 = jnp.concatenate([q_ref[f, h, pl.ds(1, 32, stride=2), :] for h in range(2)], axis=1)
    s_ref[f, 0, 8:40] = d1
    s_ref[f, 1, 8:40] = d2
    d3 = s_ref[f, 0, 9:41]
    d0 = s_ref[f, 1, 7:39]
    for k, v in enumerate((d0 - d2, d1 + d2, d2 - d1, d1 - d3)):
        u_ref[(k, *to)] = v.astype(BF)


def own_row(ok_ref, red_ref, f, r, u_ref, s_ref, q_ref):
    act = silu(red_ref[f % 2, r].astype(F32))
    if r == 0 or r == 9:
        act = act * ok_ref[r // 9]
    prep_mid(act, f, (f, r), u_ref, s_ref, q_ref)


def taps(ks_ref, g_ref, k, i):
    if k == 0 or k == 3:
        return jnp.concatenate([ks_ref[i, j, 2 * (k // 3)] for j in range(3)], axis=0)
    return g_ref[k - 1, i].reshape(768, 256)


def columns(t_ref, at, y0, y1):
    for h in range(2):
        lanes = slice(h * 128, h * 128 + 128)
        t_ref[(*at, h, pl.ds(0, 32, stride=2), slice(None))] = y0[:, lanes]
        t_ref[(*at, h, pl.ds(1, 32, stride=2), slice(None))] = y1[:, lanes]


def frames_lhs(u_ref, k, f, count, r0, rows):
    return jnp.concatenate(
        [u_ref[k, f : f + count, r0 + j : r0 + j + rows].reshape(count * rows * 32, 256) for j in range(3)], axis=1
    )


def mixed(ms, rows):
    y0 = (ms[1] + ms[2] + ms[0]).reshape(rows, 32, 256)
    y1 = (ms[1] - ms[2] - ms[3]).reshape(rows, 32, 256)
    return y0, y1


def kernel_next(ok_ref, u_in, red_ref, ks_ref, g_ref, u_ref, zl_ref, s_ref, q_ref, t_ref):
    clear_edges(s_ref)
    for r in (0, 1, 8, 9):
        for f in (2, 3):
            own_row(ok_ref, red_ref, f, r, u_ref, s_ref, q_ref)
    ms = ([], [])
    for k in range(4):
        d0 = jnp.dot(frames_lhs(u_ref, k, 2, 2, 0, 8), taps(ks_ref, g_ref, k, 0), preferred_element_type=F32)
        d1 = jnp.dot(frames_lhs(u_ref, k, 3, 1, 0, 8), taps(ks_ref, g_ref, k, 1), preferred_element_type=F32)
        ms[0].append(d0[:256] + d1)
        ms[1].append(d0[256:])
    for f in range(2):
        y0, y1 = mixed(ms[f], 8)
        for r in range(8):
            columns(t_ref, (f, r), y0[r], y1[r])
            for h in range(2):
                zl_ref[f, r, :, h * 128 : h * 128 + 128] = t_ref[f, r, h].astype(BF)


def kernel_same(ok_ref, u_in, p_ref, z_ref, ks_ref, g_ref, u_ref, red_ref, y_ref, s_ref, q_ref):
    clear_edges(s_ref)

    def joined(f, r):
        red_ref[f, r] = (p_ref[f, r] + z_ref[f, r].astype(F32)).astype(BF)
        own_row(ok_ref, red_ref, f, r, u_ref, s_ref, q_ref)

    pump = Pump([lambda f=f, r=r: joined(f, r) for r in range(10) for f in (0, 1)], 4)
    ms = ([], [])
    for k in range(4):
        d2 = jnp.dot(frames_lhs(u_ref, k, 2, 2, 0, 8), taps(ks_ref, g_ref, k, 2), preferred_element_type=F32)
        d1 = jnp.dot(frames_lhs(u_ref, k, 2, 1, 0, 8), taps(ks_ref, g_ref, k, 1), preferred_element_type=F32)
        ms[0].append(d2[:256])
        ms[1].append(d2[256:] + d1)
        pump()
    for f in range(2):
        y0, y1 = mixed(ms[f], 8)
        for r in range(8):
            columns(y_ref, (f, r), y0[r], y1[r])


def kernel_rest(u_ref, red01_ref, red23_ref, y_ref, ks_ref, g_ref, bs_ref, lat_ref, y01_ref, t_ref, out_ref, sem):
    copies = []
    for r0 in range(0, 8, STEP):
        n = STEP * 32
        ms = ([], [], [], [])
        for k in range(4):
            lhs = frames_lhs(u_ref, k, 0, 2, r0, STEP)
            e0, e1, e2 = (jnp.dot(lhs, taps(ks_ref, g_ref, k, i), preferred_element_type=F32) for i in range(3))
            ms[0].append(e2[:n])
            ms[1].append(e2[n:] + e1[:n])
            ms[2].append(e1[n:] + e0[:n])
            ms[3].append(e0[n:])
        for f in (2, 3, 0, 1):
            y0, y1 = mixed(ms[f], STEP)
            for r in range(r0, r0 + STEP):
                columns(t_ref, (f, r), y0[r - r0], y1[r - r0])
                for h in range(2):
                    lanes = slice(h * 128, h * 128 + 128)
                    v = t_ref[f, r, h] + (red01_ref, red23_ref)[f // 2][f % 2, r + 1, :, lanes].astype(F32) + bs_ref[:, lanes]
                    if f < 2:
                        y01_ref[f, r, :, lanes] = v
                    else:
                        out_ref[f - 2, r, :, lanes] = (v + y_ref[f - 2, r, h]).astype(BF)
            if f > 1:
                rows = pl.ds(r0, STEP)
                copies.append(pltpu.make_async_copy(out_ref.at[f - 2, rows], lat_ref.at[f, rows], sem.at[len(copies)]))
                copies[-1].start()
    for c in copies:
        c.wait()


def kernel_last(lat_in, y_ref, zl_ref, lat_ref, out_ref, sem):
    copies = []
    for f in range(2):
        for r in range(8):
            out_ref[f, r] = (y_ref[f, r] + zl_ref[f, r].astype(F32)).astype(BF)
        copies.append(pltpu.make_async_copy(out_ref.at[f], lat_ref.at[f], sem.at[f]))
        copies[-1].start()
    for c in copies:
        c.wait()


V = pl.BlockSpec(memory_space=pltpu.VMEM)
HBM = pl.BlockSpec(memory_space=pltpu.HBM)


def sds(*shape):
    return jax.ShapeDtypeStruct(shape, BF)


def res(*shape, dtype=BF):
    return VMEM(shape, dtype)


def keep(*xs):
    return [pltpu.with_memory_space_constraint(x, pltpu.VMEM) for x in xs]


def far(*xs):
    return [pltpu.with_memory_space_constraint(x, pltpu.HBM) for x in xs]


def call(body, ins, outs, scratch, flops, in_specs=None, out_specs=None, aliases=None):
    return pl.pallas_call(
        body,
        out_shape=outs,
        in_specs=in_specs or [V] * len(ins),
        out_specs=out_specs or [V] * len(outs),
        scratch_shapes=scratch,
        input_output_aliases=aliases or {},
        compiler_params=pltpu.CompilerParams(vmem_limit_bytes=LIMIT),
        cost_estimate=pl.CostEstimate(flops=flops, bytes_accessed=4 << 20, transcendentals=0),
    )(*ins)


def on_device(features, kf, bf, kd, bd, ks, bs):
    tm, sp = lax.axis_size("tm"), lax.axis_size("space")
    down = [(i, i + 1) for i in range(sp - 1)]
    up = [(i + 1, i) for i in range(sp - 1)]
    later = [(i, i + 1) for i in range(tm - 1)]
    at = lax.axis_index("space")
    ok = jnp.stack([at > 0, at < sp - 1]).astype(F32).reshape(2, 1, 1) * jnp.ones((1, 1, 256), F32)

    wide = [VMEM((4, 2, 80, 128), F32), VMEM((4, 128, 128), F32)]
    half = [VMEM((4, 2, 48, 256), F32), VMEM((4, 2, 64, 128), F32)]
    shift = VMEM((2, 7, 72, 128), F32)
    fshape, ushape, x2shape, u2shape = (2, 2, 11, 64, 384), (4, 2, 23, 64, 256), (4, 21, 64, 256), (4, 4, 10, 32, 256)
    yshape, rshape = (2, 8, 2, 64, 128), (2, 10, 64, 256)
    kfv, edge_dn, edge_up = call(
        kernel_load, (*keep(ok), *far(features, kf)),
        [res(3, 3, 3, 128, 128), sds(4, 4, 128, 128), sds(4, 3, 128, 128)],
        [pltpu.SemaphoreType.DMA((3,))], 100_000_000, in_specs=[V] + [HBM] * 2,
    )
    top = lax.ppermute(edge_dn, "space", down)
    bot = lax.ppermute(edge_up, "space", up)
    u, x2, w, ksv, g, kdv, bfv, bdv, bsv, f45, f23, part, red23, u2 = call(
        kernel_own, (*keep(ok, kfv), *far(features, ks, kd, bf.reshape(1, 128), bd.reshape(1, 256), bs.reshape(1, 256))),
        [
            res(*ushape), res(*x2shape), res(4, 3, 2, 256, 256), res(3, 3, 3, 256, 256), res(2, 3, 3, 256, 256),
            res(3, 3, 128, 256), res(1, 128, dtype=F32), res(1, 256, dtype=F32), res(1, 256, dtype=F32),
            *[res(*fshape)] * 2, res(*rshape), res(*rshape), res(*u2shape),
        ],
        [VMEM((4, 16, 128, 128), BF), *wide, shift, *half, pltpu.SemaphoreType.DMA((9,))], 8_000_000_000, in_specs=[V] * 2 + [HBM] * 6,
    )
    u, x2, _, part = call(
        kernel_ahead, (*keep(ok, u, x2, f45, part), top, bot, *keep(w, kdv)),
        [res(*ushape), res(*x2shape), res(*fshape), res(*rshape)],
        [*wide, shift], 2_000_000_000, aliases={1: 0, 2: 1, 3: 2, 4: 3},
    )
    zpart = lax.ppermute(part, "tm", later)
    _, red23 = call(
        kernel_late, keep(ok, u, x2, f23, red23, w, kdv, bfv, bdv), [res(*fshape), res(*rshape)],
        [shift], 2_500_000_000, aliases={3: 0, 4: 1},
    )
    u2, zl = call(
        kernel_next, keep(ok, u2, red23, ksv, g), [res(*u2shape), sds(2, 8, 64, 256)],
        [*half, VMEM(yshape, F32)], 2_000_000_000, aliases={1: 0},
    )
    zlat = lax.ppermute(zl, "tm", later)
    (p01,) = call(
        kernel_early, keep(ok, u, x2, w, kdv, bfv, bdv), [res(*rshape, dtype=F32)],
        [VMEM(fshape, BF), shift], 4_000_000_000,
    )
    u2, red01, y = call(
        kernel_same, (*keep(ok, u2, p01), zpart, *keep(ksv, g)),
        [res(*u2shape), res(*rshape), res(*yshape, dtype=F32)], half, 2_000_000_000, aliases={1: 0},
    )
    lat, y01 = call(
        kernel_rest, keep(u2, red01, red23, y, ksv, g, bsv),
        [sds(4, 8, 64, 256), res(2, 8, 64, 256, dtype=F32)],
        [VMEM((4, 8, 2, 64, 128), F32), VMEM((2, 8, 64, 256), BF), pltpu.SemaphoreType.DMA((2 * 8 // STEP,))],
        4_000_000_000, out_specs=[HBM, V],
    )
    (lat,) = call(
        kernel_last, (lat, *keep(y01), zlat), [sds(4, 8, 64, 256)],
        [VMEM((2, 8, 64, 256), BF), pltpu.SemaphoreType.DMA((2,))],
        100_000_000, in_specs=[HBM, V, V], out_specs=[HBM], aliases={0: 0},
    )
    return lat


def solution(mesh):
    in_specs = (P("tm", "space", None, None), P(), P(), P(), P(), P(), P())
    out_specs = P("tm", "space", None, None)
    return jax.shard_map(on_device, mesh=mesh, in_specs=in_specs, out_specs=out_specs, check_vma=False)
```
